256 devices in a mesh: chan: 32 (over z, x_lo, core), day: 8 (over x_hi, y).
Axes of the slice: x: 4 (x_hi: 2, x_lo: 2; x = x_hi * 2 + x_lo), y: 4, z: 8, core: 2. Of those that a mesh axis runs over, the one named last changes fastest.
Arguments:
- spectra: bfloat16 [8, 512, 2, 4096], P('day', 'chan'), may hold values from -6 to 6
- source_index: int32 [16], replicated, may hold values from 0 to 511, as said below
- interrogator: int32 [512], P('chan'), may hold values from 0 to 7, as said below
- lag_bounds: int32 [16, 2], replicated, may hold values from 0 to 256, as said below
Outputs:
- reference_stack: bfloat16 [16, 512, 256], P('day', 'chan')
- drift: float32 [8, 8], P('day')
The draws below stay inside these ranges and needn't reach their ends.
Inputs may be any that keep to these rules, and one draw needn't show every extreme that they name: `source_index`: distinct channels. Each interrogator serves one contiguous run of channels, in rising order, of at least 32 channels. `lag_bounds`: first lag below end lag, and each window spans at least 128 lags.
All inputs are finite; a program needn't handle non-finite values.
Results may differ from the reference program's by a relative error of at most 0.0065.
Values may be sent and summed in bfloat16 or wider, within the bound.
No kernel may reach another device: no remote copies, remote signals or barrier semaphores. Data moves between devices by JAX's collectives and lax.ppermute only.
A program may use at most 64 MiB of HBM per device.

```python
import math
import jax
import jax.numpy as jnp
from jax import lax

BINS = 4096
LAGS = 256
NSRC = 16
NINT = 8
CHANNELS = 512
DAYS = 8


def draw_source_index(key, part):
    return jax.random.permutation(jax.random.fold_in(key, 11), CHANNELS)[:NSRC].astype(jnp.int32)


def draw_interrogator(key, part):
    span = CHANNELS // NINT
    jitter = CHANNELS // (4 * NINT)
    steps = jnp.arange(1, NINT, dtype=jnp.int32)
    cuts = steps * span + jax.random.randint(jax.random.fold_in(key, 23), (NINT - 1,), -jitter, jitter + 1)
    channel = jnp.arange(CHANNELS, dtype=jnp.int32)
    return jnp.sum((channel[:, None] >= cuts[None, :]).astype(jnp.int32), 1).astype(jnp.int32)


def draw_lag_bounds(key, part):
    first = jax.random.randint(jax.random.fold_in(key, 31), (NSRC,), 0, LAGS // 4)
    last = LAGS - jax.random.randint(jax.random.fold_in(key, 37), (NSRC,), 0, LAGS // 4)
    first = first.at[0].set(0)
    last = last.at[0].set(LAGS)
    return jnp.stack([first, last], 1).astype(jnp.int32)


def shard_levels(own_key, shape, pieces, low, largest):
    def one(dim, blocks):
        heights = jax.random.uniform(jax.random.fold_in(jax.random.fold_in(own_key, 6), dim), (blocks,), jnp.float32, low / len(pieces), largest / len(pieces))
        return jnp.repeat(jnp.exp(heights), shape[dim] // blocks).reshape((-1,) + (1,) * (len(shape) - dim - 1))

    gain = one(*pieces[0])
    for cut in pieces[1:]:
        gain = gain * one(*cut)
    return gain


def bell_draw(rng, dims, width, limit, pieces=(), held_as=jnp.bfloat16):
    factor_of = shard_levels(rng, dims, pieces, -0.22, 0.18) if pieces else 1.0
    drawn = jax.random.normal(rng, dims, jnp.float32) * width * factor_of
    return jnp.minimum(jnp.maximum(drawn, -limit), limit).astype(held_as)


def setup_inputs(seed: int = 0) -> dict:
    streams_of = jax.random.split(jax.random.key(seed), 5)
    spectra = bell_draw(streams_of[0], (DAYS, CHANNELS, 2, BINS), 1.0, 6.0, ((0, 8), (1, 32)))
    source_index = draw_source_index(jax.random.fold_in(streams_of[4], 71), 0)
    interrogator = draw_interrogator(jax.random.fold_in(streams_of[4], 71), 0)
    lag_bounds = draw_lag_bounds(jax.random.fold_in(streams_of[4], 71), 0)
    return dict(spectra=spectra, source_index=source_index, interrogator=interrogator, lag_bounds=lag_bounds)


def lag_table(bins, lags):
    freq = jnp.arange(bins, dtype=jnp.int32)
    shift = jnp.arange(lags, dtype=jnp.int32) - lags // 2
    phase = freq[:, None] * shift[None, :] % (2 * bins)
    angle = math.pi * phase.astype(jnp.float32) / bins
    scale = 1.0 / math.sqrt(bins)
    return jnp.concatenate([jnp.cos(angle) * scale, -jnp.sin(angle) * scale], 0).astype(jnp.bfloat16)

def correlate(spec_day, source, table):
    local = spec_day.astype(jnp.float32)
    chosen = source.astype(jnp.float32)
    real_in, imag_in = (local[:, 0], local[:, 1])
    real_src, imag_src = (chosen[0][None, :], chosen[1][None, :])
    cross = jnp.concatenate([real_in * real_src + imag_in * imag_src, imag_in * real_src - real_in * imag_src], -1).astype(jnp.bfloat16)
    return jnp.dot(cross, table, preferred_element_type=jnp.float32)

def reference(spectra, source_index, interrogator, lag_bounds):
    table = lag_table(BINS, LAGS)

    def one_day(carry, spec_day):
        sources = spec_day[source_index]
        corr = lax.map(lambda source: correlate(spec_day, source, table), sources)
        return (carry + corr, corr)
    total, corr_all = lax.scan(one_day, jnp.zeros((NSRC, CHANNELS, LAGS), jnp.float32), spectra)
    reference_stack = (total / DAYS).astype(jnp.bfloat16)
    ref_float = reference_stack.astype(jnp.float32)
    lag_pos = jnp.arange(LAGS, dtype=jnp.int32)
    window = ((lag_pos[None, :] >= lag_bounds[:, 0:1]) & (lag_pos[None, :] < lag_bounds[:, 1:2])).astype(jnp.float32)
    member = (interrogator[:, None] == jnp.arange(NINT, dtype=jnp.int32)[None, :]).astype(jnp.float32)

    def drift_day(corr):
        padded = jnp.pad(corr, ((0, 0), (0, 0), (1, 1)))
        slope = 0.5 * (padded[:, :, 2:] - padded[:, :, :-2])
        weighted = window[:, None, :] * slope
        num_chan = lax.optimization_barrier(jnp.sum(weighted * (corr - ref_float), axis=(0, 2)))
        den_chan = lax.optimization_barrier(jnp.sum(weighted * slope, axis=(0, 2)))
        num = lax.optimization_barrier(jnp.sum(num_chan[:, None] * member, 0))
        den = lax.optimization_barrier(jnp.sum(den_chan[:, None] * member, 0))
        return num / (den + 1e-06)
    drift = lax.map(drift_day, corr_all)
    return (reference_stack, drift)
```

```python
import math

import jax
import jax.numpy as jnp
import numpy as np
from jax import lax
from jax.experimental import pallas as pl
from jax.experimental.pallas import tpu as pltpu
from jax.sharding import Mesh, PartitionSpec as P

LAGS = 256
NINT = 8
BINS = 4096
NSRC = 16
CH = 16
LANE = 128
BF = jnp.bfloat16
F32 = jnp.float32
CHUNKS = 8
CB = BINS // CHUNKS
VMEM = pl.BlockSpec(memory_space=pltpu.VMEM)
SMEM = pl.BlockSpec(memory_space=pltpu.SMEM)


def chan_index():
    return (lax.axis_index("z") * 2 + lax.axis_index("xlo")) * 2 + lax.axis_index("core")


def day_index():
    return lax.axis_index("xhi") * 4 + lax.axis_index("y")


def factor_tables():
    tau = np.arange(LAGS, dtype=np.int64)[None, :] - LAGS // 2
    step = np.arange(64, dtype=np.int64)[:, None]
    coarse = math.pi * ((64 * step * tau) % (2 * BINS)) / BINS
    fine = math.pi * ((step * tau) % (2 * BINS)) / BINS
    scale = 1.0 / math.sqrt(BINS)
    parts = [np.cos(coarse) * scale, np.sin(coarse) * scale, np.cos(fine), np.sin(fine)]
    return np.stack(parts).astype(np.float32)


def table_kernel(f_ref, t_ref):
    cb = f_ref[2]
    sb = f_ref[3]
    per = CB // 64

    def body(a, c):
        ca = f_ref[0, pl.ds(a, 1), :]
        sa = f_ref[1, pl.ds(a, 1), :]
        q = a // per
        r = pl.multiple_of((a % per) * 64, 64)
        t_ref[q, pl.ds(r, 64), :] = (ca * cb - sa * sb).astype(BF)
        t_ref[q, pl.ds(CB + r, 64), :] = (-(sa * cb + ca * sb)).astype(BF)
        return c

    lax.fori_loop(0, BINS // 64, body, 0)


def prepare_kernel(src_ref, x_ref, planes_ref, mine_ref, other_ref):
    base = chan_index() * CH
    core = lax.axis_index("core")
    rows = lax.broadcasted_iota(jnp.int32, (64, 32), 0)
    cols = lax.broadcasted_iota(jnp.int32, (64, 32), 1)
    want = jnp.where(rows < 32, 2 * (rows % 16) + (rows // 16) % 2, -1)
    for s in range(NSRC):
        local = src_ref[s] - base
        ok = jnp.logical_and(local >= 0, local < CH)
        first = jnp.where(ok, 2 * local, -1)
        second = jnp.where(ok, 2 * local + 1, -1)
        want = jnp.where(rows == 32 + s, first, want)
        want = jnp.where(rows == 48 + s, second, want)
    pick = (cols == want).astype(F32).astype(BF)
    half = BINS // 2

    def part(h, dst):
        lo = pl.multiple_of(h * half, half)
        for g in range(half // 512):
            off = pl.multiple_of(lo + g * 512, 512)
            got = jnp.dot(pick, x_ref[:, pl.ds(off, 512)], preferred_element_type=F32)
            planes_ref[:, pl.ds(off, 512)] = got[:32]
            srcs = got[32:].astype(BF)
            for j in range(4):
                dst[g * 4 + j] = srcs[:, j * LANE : (j + 1) * LANE]

    part(1 - core, other_ref)
    part(core, mine_ref)


def spread_kernel(p_ref, o_ref):
    n = p_ref.shape[0]
    total = p_ref[0]
    for i in range(1, n):
        total = total + p_ref[i]
    for i in range(n):
        o_ref[i] = total


def correlate_kernel(planes_ref, mine_ref, other_ref, t_ref, o_ref, cross_ref):
    core = lax.axis_index("core")

    def build(v_ref, slot, g, off):
        for j in range(CB // LANE):
            lo = pl.multiple_of(off + j * LANE, LANE)
            sr = planes_ref[0:16, pl.ds(lo, LANE)]
            si = planes_ref[16:32, pl.ds(lo, LANE)]
            v = v_ref[g * (CB // LANE) + j].astype(F32)
            for s in range(NSRC):
                vr = v[s : s + 1]
                vi = v[16 + s : 17 + s]
                cross_ref[slot, s * CH : (s + 1) * CH, j * LANE : (j + 1) * LANE] = (
                    sr * vr + si * vi
                ).astype(BF)
                cross_ref[slot, s * CH : (s + 1) * CH, CB + j * LANE : CB + (j + 1) * LANE] = (
                    si * vr - sr * vi
                ).astype(BF)

    per_half = CHUNKS // 2
    o_ref[...] = jnp.zeros_like(o_ref)
    for v_ref, h in ((mine_ref, core), (other_ref, 1 - core)):

        def body(g, c, v_ref=v_ref, h=h):
            q = h * per_half + g
            build(v_ref, 0, g, q * CB)
            o_ref[...] += jnp.dot(cross_ref[0], t_ref[q], preferred_element_type=F32)
            return c

        lax.fori_loop(0, per_half, body, 0)


def drift_kernel(bounds_ref, intr_ref, c_ref, ref_ref, o_ref):
    day = day_index()
    lane = lax.broadcasted_iota(jnp.int32, (32, LAGS), 1)
    rowi = lax.broadcasted_iota(jnp.int32, (32, LAGS), 0)
    first = jnp.where(rowi < 16, bounds_ref[2 * day, 0], bounds_ref[2 * day + 1, 0])
    last = jnp.where(rowi < 16, bounds_ref[2 * day, 1], bounds_ref[2 * day + 1, 1])
    window = jnp.logical_and(lane >= first, lane < last)
    not_last = lane < LAGS - 1
    not_first = lane > 0
    rows = lax.broadcasted_iota(jnp.int32, (32, LANE), 0) % 16
    cols = lax.broadcasted_iota(jnp.int32, (32, LANE), 1)
    kind = jnp.zeros((32, LANE), jnp.int32)
    for c in range(CH):
        kind = jnp.where(rows == c, intr_ref[c], kind)
    in_num = (cols == kind).astype(F32)
    in_den = (cols == kind + NINT).astype(F32)
    total = c_ref[0]
    for d in range(1, 8):
        total = total + c_ref[d]
    ref = (total * 0.125).astype(BF)
    ref_ref[...] = ref
    ref = ref.astype(F32)
    for d in range(8):
        corr = c_ref[d]
        ahead = jnp.where(not_last, pltpu.roll(corr, LAGS - 1, 1), 0.0)
        behind = jnp.where(not_first, pltpu.roll(corr, 1, 1), 0.0)
        slope = jnp.where(window, 0.5 * (ahead - behind), 0.0)
        num = jnp.sum(slope * (corr - ref), axis=1, keepdims=True)
        den = jnp.sum(slope * slope, axis=1, keepdims=True)
        o_ref[d] = jnp.sum(num * in_num + den * in_den, axis=0, keepdims=True)


def repeat_sum_kernel(p_ref, o_ref):
    total = jnp.sum(p_ref[...], axis=0)
    for i in range(o_ref.shape[0]):
        o_ref[i] = total


def finish_kernel(p_ref, o_ref):
    total = jnp.sum(p_ref[...], axis=0)
    o_ref[...] = total[:, :NINT] / (total[:, NINT : 2 * NINT] + 1e-06)


def call(kernel, out_shape, in_specs, name, scratch=()):
    multi = isinstance(out_shape, (list, tuple))
    return pl.pallas_call(
        kernel,
        out_shape=out_shape,
        in_specs=in_specs,
        out_specs=[VMEM] * len(out_shape) if multi else VMEM,
        scratch_shapes=list(scratch),
        compiler_params=pltpu.CompilerParams(vmem_limit_bytes=40 << 20),
        name=name,
    )


def shaped(shape, dtype):
    return jax.ShapeDtypeStruct(shape, dtype)


PAIR = [(0, 1), (1, 0)]


def per_device(spectra, source_index, interrogator, lag_bounds):
    x = spectra.reshape(2 * CH, BINS)
    piece = (16, 32, LANE)
    table = call(table_kernel, shaped((CHUNKS, 2 * CB, LAGS), BF), [VMEM], "lag_table")(
        jnp.asarray(factor_tables())
    )
    planes, mine, other = call(
        prepare_kernel,
        [shaped((32, BINS), F32), shaped(piece, BF), shaped(piece, BF)],
        [SMEM, VMEM],
        "prepare",
    )(source_index, x)
    got = lax.ppermute(other, "core", PAIR)
    parts = lax.all_to_all(mine + got, ("z", "xlo"), 0, 0)
    parts = call(spread_kernel, shaped(piece, BF), [VMEM], "spread")(parts)
    mine_half = lax.all_to_all(parts, ("z", "xlo"), 0, 0)
    other_half = lax.ppermute(mine_half, "core", PAIR)
    corr = call(
        correlate_kernel,
        shaped((NSRC * CH, LAGS), F32),
        [VMEM] * 4,
        "correlate",
        [pltpu.VMEM((1, NSRC * CH, 2 * CB), BF)],
    )(planes, mine_half, other_half, table)
    days = lax.all_to_all(corr.reshape(8, 32, LAGS), ("xhi", "y"), 0, 0)
    ref, fits = call(
        drift_kernel,
        [shaped((32, LAGS), BF), shaped((8, 1, LANE), F32)],
        [SMEM, SMEM, VMEM],
        "drift",
    )(lag_bounds, interrogator, days)
    fits = lax.all_to_all(fits, ("xhi", "y"), 0, 0)
    fits = call(repeat_sum_kernel, shaped((32, 1, LANE), F32), [VMEM], "day_fits")(fits)
    fits = lax.all_to_all(fits, ("z", "xlo", "core"), 0, 0)
    drift = call(finish_kernel, shaped((1, NINT), F32), [VMEM], "finish")(fits)
    return ref.reshape(2, CH, LAGS), drift


def solution(mesh):
    fine = Mesh(mesh.devices.reshape(8, 2, 2, 2, 4), ("z", "xlo", "core", "xhi", "y"))
    chan = ("z", "xlo", "core")
    day = ("xhi", "y")
    return jax.shard_map(
        per_device,
        mesh=fine,
        in_specs=(P(day, chan, None, None), P(), P(chan), P()),
        out_specs=(P(day, chan, None), P(day, None)),
        check_vma=False,
    )
```

```python
import math

import jax
import jax.numpy as jnp
import numpy as np
from jax import lax
from jax.experimental import pallas as pl
from jax.experimental.pallas import tpu as pltpu
from jax.sharding import Mesh, PartitionSpec as P

LAGS = 256
NINT = 8
BINS = 4096
NSRC = 16
CH = 16
LANE = 128
BF = jnp.bfloat16
F32 = jnp.float32
CHUNKS = 8
CB = BINS // CHUNKS
VMEM = pl.BlockSpec(memory_space=pltpu.VMEM)
SMEM = pl.BlockSpec(memory_space=pltpu.SMEM)


def chan_index():
    return (lax.axis_index("z") * 2 + lax.axis_index("xlo")) * 2 + lax.axis_index("core")


def day_index():
    return lax.axis_index("xhi") * 4 + lax.axis_index("y")


def factor_tables():
    tau = np.arange(LAGS, dtype=np.int64)[None, :] - LAGS // 2
    step = np.arange(64, dtype=np.int64)[:, None]
    coarse = math.pi * ((64 * step * tau) % (2 * BINS)) / BINS
    fine = math.pi * ((step * tau) % (2 * BINS)) / BINS
    scale = 1.0 / math.sqrt(BINS)
    parts = [np.cos(coarse) * scale, np.sin(coarse) * scale, np.cos(fine), np.sin(fine)]
    return np.stack(parts).astype(np.float32)


def table_kernel(f_ref, _, t_ref):
    cb = f_ref[2]
    sb = f_ref[3]
    per = CB // 64

    def body(a, c):
        ca = f_ref[0, pl.ds(a, 1), :]
        sa = f_ref[1, pl.ds(a, 1), :]
        q = a // per
        r = pl.multiple_of((a % per) * 64, 64)
        t_ref[q, pl.ds(r, 64), :] = (ca * cb - sa * sb).astype(BF)
        t_ref[q, pl.ds(CB + r, 64), :] = (-(sa * cb + ca * sb)).astype(BF)
        return c

    lax.fori_loop(0, BINS // 64, body, 0)


def prepare_kernel(
    spec_hbm,
    src_hbm,
    intr_hbm,
    bounds_hbm,
    f_hbm,
    planes_ref,
    mine_ref,
    other_ref,
    window_ref,
    member_ref,
    f_ref,
    x_ref,
    src_ref,
    intr_ref,
    bounds_ref,
    sems,
):
    copies = [
        pltpu.make_async_copy(a, b, sems.at[i])
        for i, (a, b) in enumerate(
            (
                (src_hbm, src_ref),
                (spec_hbm, x_ref),
                (intr_hbm, intr_ref),
                (bounds_hbm, bounds_ref),
                (f_hbm, f_ref),
            )
        )
    ]
    for copy in copies:
        copy.start()
    base = chan_index() * CH
    core = lax.axis_index("core")
    rows = lax.broadcasted_iota(jnp.int32, (64, 32), 0)
    cols = lax.broadcasted_iota(jnp.int32, (64, 32), 1)
    want = jnp.where(rows < 32, 2 * (rows % 16) + (rows // 16) % 2, -1)
    copies[0].wait()
    for s in range(NSRC):
        local = src_ref[s] - base
        ok = jnp.logical_and(local >= 0, local < CH)
        first = jnp.where(ok, 2 * local, -1)
        second = jnp.where(ok, 2 * local + 1, -1)
        want = jnp.where(rows == 32 + s, first, want)
        want = jnp.where(rows == 48 + s, second, want)
    pick = (cols == want).astype(F32).astype(BF)
    half = BINS // 2
    copies[1].wait()

    def part(h, dst):
        lo = pl.multiple_of(h * half, half)
        for g in range(half // 512):
            off = pl.multiple_of(lo + g * 512, 512)
            x = x_ref[:, :, pl.ds(off, 512)].reshape(2 * CH, 512)
            got = jnp.dot(pick, x, preferred_element_type=F32)
            planes_ref[:, pl.ds(off, 512)] = got[:32]
            srcs = got[32:].astype(BF)
            for j in range(4):
                dst[g * 4 + j] = srcs[:, j * LANE : (j + 1) * LANE]

    part(1 - core, other_ref)
    part(core, mine_ref)

    copies[2].wait()
    copies[3].wait()
    day = day_index()
    lane = lax.broadcasted_iota(jnp.int32, (32, LAGS), 1)
    rowi = lax.broadcasted_iota(jnp.int32, (32, LAGS), 0)
    first = jnp.where(rowi < CH, bounds_ref[0, 2 * day], bounds_ref[0, 2 * day + 1])
    last = jnp.where(rowi < CH, bounds_ref[1, 2 * day], bounds_ref[1, 2 * day + 1])
    window_ref[...] = jnp.logical_and(lane >= first, lane < last).astype(F32)
    rows = lax.broadcasted_iota(jnp.int32, (32, LANE), 0) % CH
    cols = lax.broadcasted_iota(jnp.int32, (32, LANE), 1)
    kind = jnp.zeros((32, LANE), jnp.int32)
    for c in range(CH):
        kind = jnp.where(rows == c, intr_ref[c], kind)
    member_ref[0] = (cols == kind).astype(F32)
    member_ref[1] = (cols == kind + NINT).astype(F32)
    copies[4].wait()


def spread_kernel(p_ref, o_ref):
    n = p_ref.shape[0]
    total = p_ref[0]
    for i in range(1, n):
        total = total + p_ref[i]
    for i in range(n):
        o_ref[i] = total


def build_cross(planes_ref, v_ref, cross_ref, g, off):
    for j in range(CB // LANE):
        lo = pl.multiple_of(off + j * LANE, LANE)
        sr = planes_ref[0:16, pl.ds(lo, LANE)]
        si = planes_ref[16:32, pl.ds(lo, LANE)]
        v = v_ref[g * (CB // LANE) + j].astype(F32)
        for s in range(NSRC):
            vr = v[s : s + 1]
            vi = v[16 + s : 17 + s]
            cross_ref[s * CH : (s + 1) * CH, j * LANE : (j + 1) * LANE] = (
                sr * vr + si * vi
            ).astype(BF)
            cross_ref[s * CH : (s + 1) * CH, CB + j * LANE : CB + (j + 1) * LANE] = (
                si * vr - sr * vi
            ).astype(BF)


def half_correlation(planes_ref, v_ref, t_ref, crosses, half):
    per_half = CHUNKS // 2
    total = None
    build_cross(planes_ref, v_ref, crosses[0], 0, half * per_half * CB)
    for g in range(per_half):
        q = half * per_half + g
        if g + 1 < per_half:
            build_cross(planes_ref, v_ref, crosses[(g + 1) % 2], g + 1, (q + 1) * CB)
        got = jnp.dot(crosses[g % 2][...], t_ref[q], preferred_element_type=F32)
        total = got if total is None else total + got
    return total


def first_half_kernel(planes_ref, v_ref, t_ref, o_ref, cross_a, cross_b):
    core = lax.axis_index("core")
    o_ref[...] = half_correlation(planes_ref, v_ref, t_ref, (cross_a, cross_b), core)


def second_half_kernel(planes_ref, v_ref, t_ref, first_ref, o_ref, cross_a, cross_b):
    core = lax.axis_index("core")
    total = half_correlation(planes_ref, v_ref, t_ref, (cross_a, cross_b), 1 - core)
    o_ref[...] = (first_ref[...] + total).reshape(o_ref.shape)


def drift_kernel(window_ref, member_ref, c_ref, ref_ref, o_ref):
    lane = lax.broadcasted_iota(jnp.int32, (32, LAGS), 1)
    window = window_ref[...] * 0.5
    ahead_w = jnp.where(lane < LAGS - 1, window, 0.0)
    behind_w = jnp.where(lane > 0, window, 0.0)
    in_num = member_ref[0]
    in_den = member_ref[1]
    total = c_ref[0]
    for d in range(1, 8):
        total = total + c_ref[d]
    ref = (total * 0.125).astype(BF)
    ref_ref[...] = ref
    ref = ref.astype(F32)
    for d in range(8):
        corr = c_ref[d]
        slope = pltpu.roll(corr, LAGS - 1, 1) * ahead_w - pltpu.roll(corr, 1, 1) * behind_w
        num = jnp.sum(slope * (corr - ref), axis=1, keepdims=True)
        den = jnp.sum(slope * slope, axis=1, keepdims=True)
        row = jnp.sum(num * in_num + den * in_den, axis=0, keepdims=True)
        for i in range(4):
            o_ref[d // 4, i, d % 4] = jnp.broadcast_to(row, (8, LANE))


def repeat_sum_kernel(p_ref, o_ref):
    total = jnp.sum(p_ref[...], axis=0)[:1]
    for i in range(o_ref.shape[0]):
        o_ref[i] = total


def finish_kernel(p_ref, r_ref, ref_ref, o_ref):
    ref_ref[...] = r_ref[...]
    total = jnp.sum(p_ref[...], axis=0)
    o_ref[...] = total[:, :NINT] / (total[:, NINT : 2 * NINT] + 1e-06)


def call(kernel, out_shape, in_specs, name, scratch=()):
    multi = isinstance(out_shape, (list, tuple))
    return pl.pallas_call(
        kernel,
        out_shape=out_shape,
        in_specs=in_specs,
        out_specs=[VMEM] * len(out_shape) if multi else VMEM,
        scratch_shapes=list(scratch),
        compiler_params=pltpu.CompilerParams(vmem_limit_bytes=40 << 20),
        name=name,
    )


def shaped(shape, dtype):
    return jax.ShapeDtypeStruct(shape, dtype)


PAIR = [(0, 1), (1, 0)]


def per_device(spectra, source_index, interrogator, lag_bounds):
    piece = (16, 32, LANE)
    factors = factor_tables()
    hbm = pl.BlockSpec(memory_space=pltpu.HBM)
    anywhere = pl.BlockSpec(memory_space=pl.ANY)
    planes, mine, other, window, member, factors = call(
        prepare_kernel,
        [
            shaped((32, BINS), F32),
            shaped(piece, BF),
            shaped(piece, BF),
            shaped((32, LAGS), F32),
            shaped((2, 32, LANE), F32),
            shaped(factors.shape, F32),
        ],
        [hbm] * 5,
        "prepare",
        [
            pltpu.VMEM((CH, 2, BINS), BF),
            pltpu.SMEM((NSRC,), jnp.int32),
            pltpu.SMEM((CH,), jnp.int32),
            pltpu.SMEM((2, NSRC), jnp.int32),
            pltpu.SemaphoreType.DMA((5,)),
        ],
    )(
        *(
            pltpu.with_memory_space_constraint(a, pltpu.HBM)
            for a in (
                spectra.reshape(CH, 2, BINS),
                source_index,
                interrogator,
                lag_bounds.T,
                jnp.asarray(factors),
            )
        )
    )
    got = lax.ppermute(other, "core", PAIR)
    table = call(
        table_kernel, shaped((CHUNKS, 2 * CB, LAGS), BF), [VMEM, anywhere], "lag_table"
    )(factors, planes)
    got, table = lax.optimization_barrier((got, table))
    parts = lax.all_to_all(mine + got, ("z", "xlo"), 0, 0)
    parts = call(spread_kernel, shaped(piece, BF), [VMEM], "spread")(parts)
    mine_half = lax.all_to_all(parts, ("z", "xlo"), 0, 0)
    other_half = lax.ppermute(mine_half, "core", PAIR)
    crosses = [pltpu.VMEM((NSRC * CH, 2 * CB), BF)] * 2
    first = call(
        first_half_kernel, shaped((NSRC * CH, LAGS), F32), [VMEM] * 3, "first_half", crosses
    )(planes, mine_half, table)
    corr = call(
        second_half_kernel, shaped((8, 32, LAGS), F32), [VMEM] * 4, "second_half", crosses
    )(planes, other_half, table, first)
    days = lax.all_to_all(corr, ("xhi", "y"), 0, 0)
    ref, fits = call(
        drift_kernel,
        [shaped((32, LAGS), BF), shaped((2, 4, 4, 8, LANE), F32)],
        [VMEM] * 3,
        "drift",
    )(window, member, days)
    fits = lax.all_to_all(fits.reshape(32, 8, LANE), ("xhi", "xlo", "core", "y"), 0, 0)
    fits = call(repeat_sum_kernel, shaped((8, 1, LANE), F32), [VMEM], "near_fits")(fits)
    fits = lax.all_to_all(fits, "z", 0, 0)
    ref, drift = call(
        finish_kernel,
        [shaped((32, LAGS), BF), shaped((1, NINT), F32)],
        [VMEM] * 2,
        "finish",
    )(fits, ref)
    return ref.reshape(2, CH, LAGS), drift


def solution(mesh):
    fine = Mesh(mesh.devices.reshape(8, 2, 2, 2, 4), ("z", "xlo", "core", "xhi", "y"))
    chan = ("z", "xlo", "core")
    day = ("xhi", "y")
    return jax.shard_map(
        per_device,
        mesh=fine,
        in_specs=(P(day, chan, None, None), P(), P(chan), P()),
        out_specs=(P(day, chan, None), P(day, None)),
        check_vma=False,
    )
```

```python
import math

import jax
import jax.numpy as jnp
import numpy as np
from jax import lax
from jax.experimental import pallas as pl
from jax.experimental.pallas import tpu as pltpu
from jax.sharding import Mesh, PartitionSpec as P

LAGS = 256
NINT = 8
BINS = 4096
NSRC = 16
CH = 16
LANE = 128
BF = jnp.bfloat16
F32 = jnp.float32
CHUNKS = 32
CB = BINS // CHUNKS
HALF = BINS // 2
VMEM = pl.BlockSpec(memory_space=pltpu.VMEM)
SMEM = pl.BlockSpec(memory_space=pltpu.SMEM)


def chan_index():
    return (lax.axis_index("z") * 2 + lax.axis_index("xlo")) * 2 + lax.axis_index("core")


def day_index():
    return lax.axis_index("xhi") * 4 + lax.axis_index("y")


def factor_tables():
    tau = np.arange(LAGS, dtype=np.int64)[None, :] - LAGS // 2
    coarse = 64 * np.arange(64, dtype=np.int64)[:, None] * tau
    fine = np.arange(64, dtype=np.int64)[:, None] * tau
    coarse, fine = (math.pi * (f % (2 * BINS)) / BINS for f in (coarse, fine))
    scale = 1.0 / math.sqrt(BINS)
    parts = [np.cos(coarse) * scale, -np.sin(coarse) * scale, np.cos(fine), np.sin(fine)]
    return np.concatenate(parts).astype(np.float32)


def half_range(h):
    return pl.ds(pl.multiple_of(h * HALF, HALF), HALF)


def owned_pick(src_ref):
    base = chan_index() * CH
    rows = lax.broadcasted_iota(jnp.int32, (32, 32), 0)
    cols = lax.broadcasted_iota(jnp.int32, (32, 32), 1)
    want = jnp.full((32, 32), -1, jnp.int32)
    for s in range(NSRC):
        local = src_ref[s] - base
        ok = jnp.logical_and(local >= 0, local < CH)
        first = jnp.where(ok, 2 * local, -1)
        second = jnp.where(ok, 2 * local + 1, -1)
        want = jnp.where(rows == s, first, want)
        want = jnp.where(rows == 16 + s, second, want)
    return (cols == want).astype(F32).astype(BF)


def plane_pick():
    rows = lax.broadcasted_iota(jnp.int32, (32, 32), 0)
    cols = lax.broadcasted_iota(jnp.int32, (32, 32), 1)
    return (cols == 2 * (rows % CH) + rows // CH).astype(F32).astype(BF)


def put_pieces(dst, g, srcs):
    for j in range(4):
        dst[g * 4 + j] = srcs[:, j * LANE : (j + 1) * LANE]


def other_kernel(spec_hbm, src_hbm, f_hbm, other_ref, x_ref, f_ref, raw_ref, src_ref, sems):
    load_src = pltpu.make_async_copy(src_hbm, src_ref, sems.at[0])
    load_src.start()
    part = half_range(1 - lax.axis_index("core"))
    load_x = pltpu.make_async_copy(spec_hbm.at[:, :, part], raw_ref, sems.at[1])
    load_x.start()
    load_f = pltpu.make_async_copy(f_hbm, f_ref, sems.at[2])
    load_f.start()
    load_src.wait()
    pick = owned_pick(src_ref)
    load_x.wait()
    for g in range(HALF // 512):
        at = slice(g * 512, (g + 1) * 512)
        x = raw_ref[:, :, at].reshape(2 * CH, 512)
        x_ref[:, at] = x
        put_pieces(other_ref, g, jnp.dot(pick, x, preferred_element_type=F32).astype(BF))
    load_f.wait()


def mine_kernel(
    spec_hbm,
    src_hbm,
    intr_hbm,
    bounds_hbm,
    x_ref,
    f_ref,
    mine_ref,
    t_ref,
    planes_ref,
    window_ref,
    member_ref,
    raw_ref,
    src_ref,
    intr_ref,
    bounds_ref,
    sems,
):
    core = lax.axis_index("core")
    copies = [
        pltpu.make_async_copy(a, b, sems.at[i])
        for i, (a, b) in enumerate(
            (
                (spec_hbm.at[:, :, half_range(core)], raw_ref),
                (src_hbm, src_ref),
                (intr_hbm, intr_ref),
                (bounds_hbm, bounds_ref),
            )
        )
    ]
    for copy in copies:
        copy.start()
    planes = plane_pick()

    def put_planes(h, g, got):
        off = pl.multiple_of(h * HALF + g * 512, 512)
        planes_ref[:, pl.ds(off, 512)] = got

    for g in range(HALF // 512):
        x = x_ref[:, g * 512 : (g + 1) * 512]
        put_planes(1 - core, g, jnp.dot(planes, x, preferred_element_type=F32))

    def body(a, c):
        ca = f_ref[pl.ds(core * 32 + a, 1), :]
        sa = f_ref[pl.ds(64 + core * 32 + a, 1), :]
        q = a // (CB // 64)
        for i in range(0, 64, 16):
            r = pl.multiple_of((a % (CB // 64)) * 64 + i, 16)
            cb = f_ref[128 + i : 144 + i]
            sb = f_ref[192 + i : 208 + i]
            t_ref[q, pl.ds(r, 16), :] = (ca * cb + sa * sb).astype(BF)
            t_ref[q, pl.ds(CB + r, 16), :] = (sa * cb - ca * sb).astype(BF)
        return c

    lax.fori_loop(0, HALF // 64, body, 0, unroll=2)
    for copy in copies:
        copy.wait()
    owned = owned_pick(src_ref)
    for g in range(HALF // 512):
        x = raw_ref[:, :, g * 512 : (g + 1) * 512].reshape(2 * CH, 512)
        put_pieces(mine_ref, g, jnp.dot(owned, x, preferred_element_type=F32).astype(BF))
        put_planes(core, g, jnp.dot(planes, x, preferred_element_type=F32))
    day = day_index()
    lane = lax.broadcasted_iota(jnp.int32, (32, LAGS), 1)
    rowi = lax.broadcasted_iota(jnp.int32, (32, LAGS), 0)
    first = jnp.where(rowi < CH, bounds_ref[0, 2 * day], bounds_ref[0, 2 * day + 1])
    last = jnp.where(rowi < CH, bounds_ref[1, 2 * day], bounds_ref[1, 2 * day + 1])
    window_ref[...] = jnp.logical_and(lane >= first, lane < last).astype(F32)
    rows = lax.broadcasted_iota(jnp.int32, (32, LANE), 0) % CH
    cols = lax.broadcasted_iota(jnp.int32, (32, LANE), 1)
    kind = jnp.zeros((32, LANE), jnp.int32)
    for c in range(CH):
        kind = jnp.where(rows == c, intr_ref[c], kind)
    member_ref[0] = (cols == kind).astype(F32)
    member_ref[1] = (cols == kind + NINT).astype(F32)


def other_table_kernel(t_ref, _, o_ref):
    lag = lax.broadcasted_iota(jnp.int32, (2 * 8, LAGS), 1) % 4
    turn = 1.0 - 2.0 * lax.axis_index("core").astype(F32)
    even = jnp.where(lag == 0, 1.0, jnp.where(lag == 2, -1.0, 0.0)).astype(BF)
    odd = (jnp.where(lag == 1, 1.0, jnp.where(lag == 3, -1.0, 0.0)) * turn).astype(BF)

    def body(q, c):
        for r in range(0, CB, 16):
            cos = t_ref[q, r : r + 16, :]
            sin = t_ref[q, CB + r : CB + r + 16, :]
            o_ref[q, r : r + 16, :] = cos * even + sin * odd
            o_ref[q, CB + r : CB + r + 16, :] = sin * even - cos * odd
        return c

    lax.fori_loop(0, CHUNKS // 2, body, 0)


def spread_kernel(p_ref, o_ref):
    n = p_ref.shape[0]
    total = p_ref[0]
    for i in range(1, n):
        total = total + p_ref[i]
    for i in range(n):
        o_ref[i] = total


def build_cross(planes_ref, v_ref, cross_ref, g, off):
    for j in range(CB // LANE):
        lo = pl.multiple_of(off + j * LANE, LANE)
        sr = [planes_ref[8 * i : 8 * i + 8, pl.ds(lo, LANE)] for i in range(2)]
        si = [planes_ref[16 + 8 * i : 24 + 8 * i, pl.ds(lo, LANE)] for i in range(2)]
        for s in range(NSRC):
            vr = v_ref[g * (CB // LANE) + j, pl.ds(s, 8, stride=0), :]
            vi = v_ref[g * (CB // LANE) + j, pl.ds(16 + s, 8, stride=0), :]
            xr = jnp.concatenate([a * vr + b * vi for a, b in zip(sr, si)], 0)
            xi = jnp.concatenate([b * vr - a * vi for a, b in zip(sr, si)], 0)
            row = slice(s * CH, (s + 1) * CH)
            cross_ref[row, j * LANE : (j + 1) * LANE] = xr.astype(BF)
            cross_ref[row, CB + j * LANE : CB + (j + 1) * LANE] = xi.astype(BF)


def half_correlation(planes_ref, v_ref, t_ref, cross_ref, wide_ref, half):
    per_half = CHUNKS // 2
    wide_ref[...] = v_ref[...].astype(F32)
    total = None
    for g in range(per_half):
        build_cross(planes_ref, wide_ref, cross_ref, g, (half * per_half + g) * CB)
        got = jnp.dot(cross_ref[...], t_ref[g], preferred_element_type=F32)
        total = got if total is None else total + got
    return total


def first_half_kernel(planes_ref, v_ref, t_ref, o_ref, cross_ref, wide_ref):
    core = lax.axis_index("core")
    o_ref[...] = half_correlation(planes_ref, v_ref, t_ref, cross_ref, wide_ref, core)


def second_half_kernel(planes_ref, v_ref, t_ref, first_ref, o_ref, cross_ref, wide_ref):
    core = lax.axis_index("core")
    total = half_correlation(planes_ref, v_ref, t_ref, cross_ref, wide_ref, 1 - core)
    o_ref[...] = (first_ref[...] + total).reshape(o_ref.shape)


def drift_kernel(window_ref, member_ref, c_ref, ref_ref, o_ref):
    lane = lax.broadcasted_iota(jnp.int32, (32, LAGS), 1)
    window = window_ref[...] * 0.5
    ahead_w = jnp.where(lane < LAGS - 1, window, 0.0)
    behind_w = jnp.where(lane > 0, window, 0.0)
    in_num = member_ref[0]
    in_den = member_ref[1]
    total = c_ref[0]
    for d in range(1, 8):
        total = total + c_ref[d]
    ref = (total * 0.125).astype(BF)
    ref_ref[...] = ref
    ref = ref.astype(F32)
    for d in range(8):
        corr = c_ref[d]
        slope = pltpu.roll(corr, LAGS - 1, 1) * ahead_w - pltpu.roll(corr, 1, 1) * behind_w
        num = jnp.sum(slope * (corr - ref), axis=1, keepdims=True)
        den = jnp.sum(slope * slope, axis=1, keepdims=True)
        rows = num * in_num + den * in_den
        rows = (rows[0:8] + rows[8:16]) + (rows[16:24] + rows[24:32])
        for i in range(4):
            o_ref[d // 4, i, d % 4] = rows


def repeat_sum_kernel(p_ref, o_ref):
    total = jnp.sum(jnp.sum(p_ref[...], axis=0), axis=0, keepdims=True)
    for i in range(o_ref.shape[0]):
        o_ref[i] = total


def finish_kernel(p_ref, r_ref, ref_ref, o_ref):
    ref_ref[...] = r_ref[...]
    total = jnp.sum(p_ref[...], axis=0)
    o_ref[...] = total[:, :NINT] / (total[:, NINT : 2 * NINT] + 1e-06)


def call(kernel, out_shape, in_specs, name, scratch=()):
    multi = isinstance(out_shape, (list, tuple))
    return pl.pallas_call(
        kernel,
        out_shape=out_shape,
        in_specs=in_specs,
        out_specs=[VMEM] * len(out_shape) if multi else VMEM,
        scratch_shapes=list(scratch),
        compiler_params=pltpu.CompilerParams(vmem_limit_bytes=16 << 20),
        name=name,
    )


def shaped(shape, dtype):
    return jax.ShapeDtypeStruct(shape, dtype)


PAIR = [(0, 1), (1, 0)]


def per_device(spectra, source_index, interrogator, lag_bounds):
    piece = (16, 32, LANE)
    factors = factor_tables()
    hbm = pl.BlockSpec(memory_space=pltpu.HBM)

    def keep(a):
        return pltpu.with_memory_space_constraint(a, pltpu.HBM)

    spec = keep(spectra.reshape(CH, 2, BINS))
    source_index = keep(source_index)
    half_table = (CHUNKS // 2, 2 * CB, LAGS)
    raw = pltpu.VMEM((CH, 2, HALF), BF)
    other, x, factors = call(
        other_kernel,
        [shaped(piece, BF), shaped((2 * CH, HALF), BF), shaped(factors.shape, F32)],
        [hbm] * 3,
        "other",
        [raw, pltpu.SMEM((NSRC,), jnp.int32), pltpu.SemaphoreType.DMA((3,))],
    )(spec, source_index, keep(jnp.asarray(factors)))
    got = lax.ppermute(other, "core", PAIR)
    mine, table, planes, window, member = call(
        mine_kernel,
        [
            shaped(piece, BF),
            shaped(half_table, BF),
            shaped((32, BINS), F32),
            shaped((32, LAGS), F32),
            shaped((2, 32, LANE), F32),
        ],
        [hbm] * 4 + [VMEM] * 2,
        "mine",
        [
            raw,
            pltpu.SMEM((NSRC,), jnp.int32),
            pltpu.SMEM((CH,), jnp.int32),
            pltpu.SMEM((2, NSRC), jnp.int32),
            pltpu.SemaphoreType.DMA((4,)),
        ],
    )(spec, source_index, keep(interrogator), keep(lag_bounds.T), x, factors)
    parts = lax.all_to_all(mine + got, ("z", "xlo"), 0, 0)
    parts = call(spread_kernel, shaped(piece, BF), [VMEM], "spread")(parts)
    mine_half = lax.all_to_all(parts, ("z", "xlo"), 0, 0)
    other_half = lax.ppermute(mine_half, "core", PAIR)
    crosses = [pltpu.VMEM((NSRC * CH, 2 * CB), BF), pltpu.VMEM(piece, F32)]
    first = call(
        first_half_kernel, shaped((NSRC * CH, LAGS), F32), [VMEM] * 3, "first_half", crosses
    )(planes, mine_half, table)
    other_table = call(
        other_table_kernel,
        shaped(half_table, BF),
        [VMEM, pl.BlockSpec(memory_space=pl.ANY)],
        "other_table",
    )(table, first)
    other_half, other_table = lax.optimization_barrier((other_half, other_table))
    corr = call(
        second_half_kernel, shaped((8, 32, LAGS), F32), [VMEM] * 4, "second_half", crosses
    )(planes, other_half, other_table, first)
    days = lax.all_to_all(corr, ("xhi", "y"), 0, 0)
    ref, fits = call(
        drift_kernel,
        [shaped((32, LAGS), BF), shaped((2, 4, 4, 8, LANE), F32)],
        [VMEM] * 3,
        "drift",
    )(window, member, days)
    fits = lax.all_to_all(fits.reshape(32, 8, LANE), ("xhi", "xlo", "core", "y"), 0, 0)
    fits = call(repeat_sum_kernel, shaped((8, 1, LANE), F32), [VMEM], "near_fits")(fits)
    fits = lax.all_to_all(fits, "z", 0, 0)
    ref, drift = call(
        finish_kernel,
        [shaped((32, LAGS), BF), shaped((1, NINT), F32)],
        [VMEM] * 2,
        "finish",
    )(fits, ref)
    return ref.reshape(2, CH, LAGS), drift


def solution(mesh):
    fine = Mesh(mesh.devices.reshape(8, 2, 2, 2, 4), ("z", "xlo", "core", "xhi", "y"))
    chan = ("z", "xlo", "core")
    day = ("xhi", "y")
    return jax.shard_map(
        per_device,
        mesh=fine,
        in_specs=(P(day, chan, None, None), P(), P(chan), P()),
        out_specs=(P(day, chan, None), P(day, None)),
        check_vma=False,
    )
```

```python
import math

import jax
import jax.numpy as jnp
import numpy as np
from jax import lax
from jax.experimental import pallas as pl
from jax.experimental.pallas import tpu as pltpu
from jax.sharding import Mesh, PartitionSpec as P

LAGS = 256
NINT = 8
BINS = 4096
NSRC = 16
CH = 16
LANE = 128
BF = jnp.bfloat16
F32 = jnp.float32
CHUNKS = 32
CB = BINS // CHUNKS
HALF = BINS // 2
VMEM = pl.BlockSpec(memory_space=pltpu.VMEM)
SMEM = pl.BlockSpec(memory_space=pltpu.SMEM)


def chan_index():
    return (lax.axis_index("z") * 2 + lax.axis_index("xlo")) * 2 + lax.axis_index("core")


def day_index():
    return lax.axis_index("xhi") * 4 + lax.axis_index("y")


def factor_tables():
    tau = np.arange(LAGS, dtype=np.int64)[None, :] - LAGS // 2
    coarse = 64 * np.arange(64, dtype=np.int64)[:, None] * tau
    fine = np.arange(64, dtype=np.int64)[:, None] * tau
    coarse, fine = (math.pi * (f % (2 * BINS)) / BINS for f in (coarse, fine))
    scale = 1.0 / math.sqrt(BINS)
    parts = [np.cos(coarse) * scale, -np.sin(coarse) * scale, np.cos(fine), np.sin(fine)]
    return np.concatenate(parts).astype(np.float32)


def half_range(h):
    return pl.ds(pl.multiple_of(h * HALF, HALF), HALF)


def owned_pick(src_ref):
    base = chan_index() * CH
    rows = lax.broadcasted_iota(jnp.int32, (32, 32), 0)
    cols = lax.broadcasted_iota(jnp.int32, (32, 32), 1)
    want = jnp.full((32, 32), -1, jnp.int32)
    for s in range(NSRC):
        local = src_ref[s] - base
        ok = jnp.logical_and(local >= 0, local < CH)
        first = jnp.where(ok, 2 * local, -1)
        second = jnp.where(ok, 2 * local + 1, -1)
        want = jnp.where(rows == s, first, want)
        want = jnp.where(rows == 16 + s, second, want)
    return (cols == want).astype(F32).astype(BF)


def plane_pick():
    rows = lax.broadcasted_iota(jnp.int32, (32, 32), 0)
    cols = lax.broadcasted_iota(jnp.int32, (32, 32), 1)
    return (cols == 2 * (rows % CH) + rows // CH).astype(F32).astype(BF)


def put_pieces(dst, g, srcs):
    for j in range(4):
        dst[g * 4 + j] = srcs[:, j * LANE : (j + 1) * LANE]


def other_kernel(spec_hbm, src_hbm, f_hbm, other_ref, x_ref, f_ref, raw_ref, src_ref, sems):
    load_src = pltpu.make_async_copy(src_hbm, src_ref, sems.at[0])
    load_src.start()
    part = half_range(1 - lax.axis_index("core"))
    load_x = pltpu.make_async_copy(spec_hbm.at[:, :, part], raw_ref, sems.at[1])
    load_x.start()
    load_f = pltpu.make_async_copy(f_hbm, f_ref, sems.at[2])
    load_f.start()
    load_src.wait()
    pick = owned_pick(src_ref)
    load_x.wait()
    for g in range(HALF // 512):
        at = slice(g * 512, (g + 1) * 512)
        x = raw_ref[:, :, at].reshape(2 * CH, 512)
        x_ref[:, at] = x
        put_pieces(other_ref, g, jnp.dot(pick, x, preferred_element_type=F32).astype(BF))
    load_f.wait()


def mine_kernel(
    spec_hbm,
    src_hbm,
    intr_hbm,
    bounds_hbm,
    x_ref,
    f_ref,
    mine_ref,
    t_ref,
    planes_ref,
    window_ref,
    member_ref,
    raw_ref,
    src_ref,
    intr_ref,
    bounds_ref,
    sems,
):
    core = lax.axis_index("core")
    copies = [
        pltpu.make_async_copy(a, b, sems.at[i])
        for i, (a, b) in enumerate(
            (
                (spec_hbm.at[:, :, half_range(core)], raw_ref),
                (src_hbm, src_ref),
                (intr_hbm, intr_ref),
                (bounds_hbm, bounds_ref),
            )
        )
    ]
    for copy in copies:
        copy.start()
    planes = plane_pick()

    def put_planes(h, g, got):
        off = pl.multiple_of(h * HALF + g * 512, 512)
        planes_ref[:, pl.ds(off, 512)] = got

    for g in range(HALF // 512):
        x = x_ref[:, g * 512 : (g + 1) * 512]
        put_planes(1 - core, g, jnp.dot(planes, x, preferred_element_type=F32))

    def body(a, c):
        ca = f_ref[pl.ds(core * 32 + a, 1), :]
        sa = f_ref[pl.ds(64 + core * 32 + a, 1), :]
        q = a // (CB // 64)
        for i in range(0, 64, 16):
            r = pl.multiple_of((a % (CB // 64)) * 64 + i, 16)
            cb = f_ref[128 + i : 144 + i]
            sb = f_ref[192 + i : 208 + i]
            t_ref[q, pl.ds(r, 16), :] = (ca * cb + sa * sb).astype(BF)
            t_ref[q, pl.ds(CB + r, 16), :] = (sa * cb - ca * sb).astype(BF)
        return c

    lax.fori_loop(0, HALF // 64, body, 0, unroll=2)
    for copy in copies:
        copy.wait()
    owned = owned_pick(src_ref)
    for g in range(HALF // 512):
        x = raw_ref[:, :, g * 512 : (g + 1) * 512].reshape(2 * CH, 512)
        put_pieces(mine_ref, g, jnp.dot(owned, x, preferred_element_type=F32).astype(BF))
        put_planes(core, g, jnp.dot(planes, x, preferred_element_type=F32))
    day = day_index()
    lane = lax.broadcasted_iota(jnp.int32, (32, LAGS), 1)
    rowi = lax.broadcasted_iota(jnp.int32, (32, LAGS), 0)
    first = jnp.where(rowi < CH, bounds_ref[0, 2 * day], bounds_ref[0, 2 * day + 1])
    last = jnp.where(rowi < CH, bounds_ref[1, 2 * day], bounds_ref[1, 2 * day + 1])
    window_ref[...] = jnp.logical_and(lane >= first, lane < last).astype(F32)
    rows = lax.broadcasted_iota(jnp.int32, (32, LANE), 0) % CH
    cols = lax.broadcasted_iota(jnp.int32, (32, LANE), 1)
    kind = jnp.zeros((32, LANE), jnp.int32)
    for c in range(CH):
        kind = jnp.where(rows == c, intr_ref[c], kind)
    member_ref[0] = (cols == kind).astype(F32)
    member_ref[1] = (cols == kind + NINT).astype(F32)


def other_table_kernel(t_ref, _, o_ref):
    lag = lax.broadcasted_iota(jnp.int32, (2 * 8, LAGS), 1) % 4
    turn = 1.0 - 2.0 * lax.axis_index("core").astype(F32)
    even = jnp.where(lag == 0, 1.0, jnp.where(lag == 2, -1.0, 0.0)).astype(BF)
    odd = (jnp.where(lag == 1, 1.0, jnp.where(lag == 3, -1.0, 0.0)) * turn).astype(BF)

    def body(q, c):
        for r in range(0, CB, 16):
            cos = t_ref[q, r : r + 16, :]
            sin = t_ref[q, CB + r : CB + r + 16, :]
            o_ref[q, r : r + 16, :] = cos * even + sin * odd
            o_ref[q, CB + r : CB + r + 16, :] = sin * even - cos * odd
        return c

    lax.fori_loop(0, CHUNKS // 2, body, 0)


def spread_kernel(p_ref, o_ref):
    n = p_ref.shape[0]
    total = p_ref[0]
    for i in range(1, n):
        total = total + p_ref[i]
    for i in range(n):
        o_ref[i] = total


def build_cross(planes_ref, v_ref, cross_ref, g, off):
    for j in range(CB // LANE):
        lo = pl.multiple_of(off + j * LANE, LANE)
        sr = [planes_ref[8 * i : 8 * i + 8, pl.ds(lo, LANE)] for i in range(2)]
        si = [planes_ref[16 + 8 * i : 24 + 8 * i, pl.ds(lo, LANE)] for i in range(2)]
        for s in range(NSRC):
            vr = v_ref[g * (CB // LANE) + j, pl.ds(s, 8, stride=0), :]
            vi = v_ref[g * (CB // LANE) + j, pl.ds(16 + s, 8, stride=0), :]
            xr = jnp.concatenate([a * vr + b * vi for a, b in zip(sr, si)], 0)
            xi = jnp.concatenate([b * vr - a * vi for a, b in zip(sr, si)], 0)
            row = slice(s * CH, (s + 1) * CH)
            cross_ref[row, j * LANE : (j + 1) * LANE] = xr.astype(BF)
            cross_ref[row, CB + j * LANE : CB + (j + 1) * LANE] = xi.astype(BF)


def half_correlation(planes_ref, v_ref, t_ref, cross_ref, wide_ref, half):
    per_half = CHUNKS // 2
    wide_ref[...] = v_ref[...].astype(F32)
    total = None
    for g in range(per_half):
        build_cross(planes_ref, wide_ref, cross_ref, g, (half * per_half + g) * CB)
        got = jnp.dot(cross_ref[...], t_ref[g], preferred_element_type=F32)
        total = got if total is None else total + got
    return total


def first_half_kernel(planes_ref, v_ref, t_ref, o_ref, cross_ref, wide_ref):
    core = lax.axis_index("core")
    o_ref[...] = half_correlation(planes_ref, v_ref, t_ref, cross_ref, wide_ref, core)


def second_half_kernel(planes_ref, v_ref, t_ref, first_ref, o_ref, cross_ref, wide_ref):
    core = lax.axis_index("core")
    total = half_correlation(planes_ref, v_ref, t_ref, cross_ref, wide_ref, 1 - core)
    o_ref[...] = (first_ref[...] + total).reshape(o_ref.shape)


def drift_kernel(window_ref, member_ref, c_ref, ref_ref, o_ref):
    lane = lax.broadcasted_iota(jnp.int32, (32, LAGS), 1)
    window = window_ref[...] * 0.5
    ahead_w = jnp.where(lane < LAGS - 1, window, 0.0)
    behind_w = jnp.where(lane > 0, window, 0.0)
    in_num = member_ref[0]
    in_den = member_ref[1]
    total = c_ref[0]
    for d in range(1, 8):
        total = total + c_ref[d]
    ref = (total * 0.125).astype(BF)
    ref_ref[...] = ref
    ref = ref.astype(F32)
    for d in range(8):
        corr = c_ref[d]
        slope = pltpu.roll(corr, LAGS - 1, 1) * ahead_w - pltpu.roll(corr, 1, 1) * behind_w
        num = jnp.sum(slope * (corr - ref), axis=1, keepdims=True)
        den = jnp.sum(slope * slope, axis=1, keepdims=True)
        rows = num * in_num + den * in_den
        rows = (rows[0:8] + rows[8:16]) + (rows[16:24] + rows[24:32])
        for i in range(4):
            o_ref[d // 4, i, d % 4] = rows


def repeat_sum_kernel(p_ref, o_ref):
    total = jnp.sum(jnp.sum(p_ref[...], axis=0), axis=0, keepdims=True)
    for i in range(o_ref.shape[0]):
        o_ref[i] = total


def finish_kernel(p_ref, r_ref, ref_ref, o_ref):
    ref_ref[...] = r_ref[...]
    total = jnp.sum(p_ref[...], axis=0)
    o_ref[...] = total[:, :NINT] / (total[:, NINT : 2 * NINT] + 1e-06)


def call(kernel, out_shape, in_specs, name, scratch=()):
    multi = isinstance(out_shape, (list, tuple))
    return pl.pallas_call(
        kernel,
        out_shape=out_shape,
        in_specs=in_specs,
        out_specs=[VMEM] * len(out_shape) if multi else VMEM,
        scratch_shapes=list(scratch),
        compiler_params=pltpu.CompilerParams(vmem_limit_bytes=16 << 20),
        name=name,
    )


def shaped(shape, dtype):
    return jax.ShapeDtypeStruct(shape, dtype)


PAIR = [(0, 1), (1, 0)]


def per_device(spectra, source_index, interrogator, lag_bounds):
    piece = (16, 32, LANE)
    factors = factor_tables()
    hbm = pl.BlockSpec(memory_space=pltpu.HBM)

    def keep(a):
        return pltpu.with_memory_space_constraint(a, pltpu.HBM)

    spec = keep(spectra.reshape(CH, 2, BINS))
    source_index = keep(source_index)
    half_table = (CHUNKS // 2, 2 * CB, LAGS)
    raw = pltpu.VMEM((CH, 2, HALF), BF)
    other, x, factors = call(
        other_kernel,
        [shaped(piece, BF), shaped((2 * CH, HALF), BF), shaped(factors.shape, F32)],
        [hbm] * 3,
        "other",
        [raw, pltpu.SMEM((NSRC,), jnp.int32), pltpu.SemaphoreType.DMA((3,))],
    )(spec, source_index, keep(jnp.asarray(factors)))
    got = lax.ppermute(other, "core", PAIR)
    mine, table, planes, window, member = call(
        mine_kernel,
        [
            shaped(piece, BF),
            shaped(half_table, BF),
            shaped((32, BINS), F32),
            shaped((32, LAGS), F32),
            shaped((2, 32, LANE), F32),
        ],
        [hbm] * 4 + [VMEM] * 2,
        "mine",
        [
            raw,
            pltpu.SMEM((NSRC,), jnp.int32),
            pltpu.SMEM((CH,), jnp.int32),
            pltpu.SMEM((2, NSRC), jnp.int32),
            pltpu.SemaphoreType.DMA((4,)),
        ],
    )(spec, source_index, keep(interrogator), keep(lag_bounds.T), x, factors)
    parts = lax.all_to_all(mine + got, ("xlo", "z"), 0, 0)
    parts = call(spread_kernel, shaped(piece, BF), [VMEM], "spread")(parts)
    mine_half = lax.all_to_all(parts, ("xlo", "z"), 0, 0)
    other_half = lax.ppermute(mine_half, "core", PAIR)
    crosses = [pltpu.VMEM((NSRC * CH, 2 * CB), BF), pltpu.VMEM(piece, F32)]
    first = call(
        first_half_kernel, shaped((NSRC * CH, LAGS), F32), [VMEM] * 3, "first_half", crosses
    )(planes, mine_half, table)
    other_table = call(
        other_table_kernel,
        shaped(half_table, BF),
        [VMEM, pl.BlockSpec(memory_space=pl.ANY)],
        "other_table",
    )(table, first)
    other_half, other_table = lax.optimization_barrier((other_half, other_table))
    corr = call(
        second_half_kernel, shaped((8, 32, LAGS), F32), [VMEM] * 4, "second_half", crosses
    )(planes, other_half, other_table, first)
    days = lax.all_to_all(corr, ("xhi", "y"), 0, 0)
    ref, fits = call(
        drift_kernel,
        [shaped((32, LAGS), BF), shaped((2, 4, 4, 8, LANE), F32)],
        [VMEM] * 3,
        "drift",
    )(window, member, days)
    fits = lax.all_to_all(fits.reshape(32, 8, LANE), ("xhi", "xlo", "core", "y"), 0, 0)
    fits = call(repeat_sum_kernel, shaped((8, 1, LANE), F32), [VMEM], "near_fits")(fits)
    fits = lax.all_to_all(fits, "z", 0, 0)
    ref, drift = call(
        finish_kernel,
        [shaped((32, LAGS), BF), shaped((1, NINT), F32)],
        [VMEM] * 2,
        "finish",
    )(fits, ref)
    return ref.reshape(2, CH, LAGS), drift


def solution(mesh):
    fine = Mesh(mesh.devices.reshape(8, 2, 2, 2, 4), ("z", "xlo", "core", "xhi", "y"))
    chan = ("z", "xlo", "core")
    day = ("xhi", "y")
    return jax.shard_map(
        per_device,
        mesh=fine,
        in_specs=(P(day, chan, None, None), P(), P(chan), P()),
        out_specs=(P(day, chan, None), P(day, None)),
        check_vma=False,
    )
```

```python
import math

import jax
import jax.numpy as jnp
import numpy as np
from jax import lax
from jax.experimental import pallas as pl
from jax.experimental.pallas import tpu as pltpu
from jax.sharding import Mesh, PartitionSpec as P

LAGS = 256
NINT = 8
BINS = 4096
NSRC = 16
CH = 16
LANE = 128
BF = jnp.bfloat16
F32 = jnp.float32
CHUNKS = 32
CB = BINS // CHUNKS
HALF = BINS // 2
VMEM = pl.BlockSpec(memory_space=pltpu.VMEM)
SMEM = pl.BlockSpec(memory_space=pltpu.SMEM)


def chan_index():
    return (lax.axis_index("z") * 2 + lax.axis_index("xlo")) * 2 + lax.axis_index("core")


def day_index():
    return lax.axis_index("xhi") * 4 + lax.axis_index("y")


def factor_tables():
    tau = np.arange(LAGS, dtype=np.int64)[None, :] - LAGS // 2
    coarse = 64 * np.arange(64, dtype=np.int64)[:, None] * tau
    fine = np.arange(64, dtype=np.int64)[:, None] * tau
    coarse, fine = (math.pi * (f % (2 * BINS)) / BINS for f in (coarse, fine))
    scale = 1.0 / math.sqrt(BINS)
    parts = [np.cos(coarse) * scale, -np.sin(coarse) * scale, np.cos(fine), np.sin(fine)]
    return np.concatenate(parts).astype(np.float32)


def half_range(h):
    return pl.ds(pl.multiple_of(h * HALF, HALF), HALF)


def owned_pick(src_ref):
    base = chan_index() * CH
    rows = lax.broadcasted_iota(jnp.int32, (32, 32), 0)
    cols = lax.broadcasted_iota(jnp.int32, (32, 32), 1)
    want = jnp.full((32, 32), -1, jnp.int32)
    for s in range(NSRC):
        local = src_ref[s] - base
        ok = jnp.logical_and(local >= 0, local < CH)
        first = jnp.where(ok, 2 * local, -1)
        second = jnp.where(ok, 2 * local + 1, -1)
        want = jnp.where(rows == s, first, want)
        want = jnp.where(rows == 16 + s, second, want)
    return (cols == want).astype(F32).astype(BF)


def plane_pick():
    rows = lax.broadcasted_iota(jnp.int32, (32, 32), 0)
    cols = lax.broadcasted_iota(jnp.int32, (32, 32), 1)
    return (cols == 2 * (rows % CH) + rows // CH).astype(F32).astype(BF)


def put_pieces(dst, g, srcs):
    for j in range(4):
        dst[g * 4 + j] = srcs[:, j * LANE : (j + 1) * LANE]


def other_kernel(spec_hbm, src_hbm, f_hbm, other_ref, x_ref, f_ref, raw_ref, src_ref, sems):
    load_src = pltpu.make_async_copy(src_hbm, src_ref, sems.at[0])
    load_src.start()
    part = half_range(1 - lax.axis_index("core"))
    load_x = pltpu.make_async_copy(spec_hbm.at[:, :, part], raw_ref, sems.at[1])
    load_x.start()
    load_f = pltpu.make_async_copy(f_hbm, f_ref, sems.at[2])
    load_f.start()
    load_src.wait()
    pick = owned_pick(src_ref)
    load_x.wait()
    for g in range(HALF // 512):
        at = slice(g * 512, (g + 1) * 512)
        x = raw_ref[:, :, at].reshape(2 * CH, 512)
        x_ref[:, at] = x
        put_pieces(other_ref, g, jnp.dot(pick, x, preferred_element_type=F32).astype(BF))
    load_f.wait()


def mine_kernel(
    spec_hbm,
    src_hbm,
    intr_hbm,
    bounds_hbm,
    x_ref,
    f_ref,
    mine_ref,
    t_ref,
    planes_ref,
    window_ref,
    member_ref,
    raw_ref,
    src_ref,
    intr_ref,
    bounds_ref,
    sems,
):
    core = lax.axis_index("core")
    copies = [
        pltpu.make_async_copy(a, b, sems.at[i])
        for i, (a, b) in enumerate(
            (
                (spec_hbm.at[:, :, half_range(core)], raw_ref),
                (src_hbm, src_ref),
                (intr_hbm, intr_ref),
                (bounds_hbm, bounds_ref),
            )
        )
    ]
    for copy in copies:
        copy.start()
    planes = plane_pick()

    def put_planes(h, g, got):
        off = pl.multiple_of(h * HALF + g * 512, 512)
        planes_ref[:, pl.ds(off, 512)] = got

    for g in range(HALF // 512):
        x = x_ref[:, g * 512 : (g + 1) * 512]
        put_planes(1 - core, g, jnp.dot(planes, x, preferred_element_type=F32))

    def body(a, c):
        ca = f_ref[pl.ds(core * 32 + a, 1), :]
        sa = f_ref[pl.ds(64 + core * 32 + a, 1), :]
        q = a // (CB // 64)
        for i in range(0, 64, 16):
            r = pl.multiple_of((a % (CB // 64)) * 64 + i, 16)
            cb = f_ref[128 + i : 144 + i]
            sb = f_ref[192 + i : 208 + i]
            t_ref[q, pl.ds(r, 16), :] = (ca * cb + sa * sb).astype(BF)
            t_ref[q, pl.ds(CB + r, 16), :] = (sa * cb - ca * sb).astype(BF)
        return c

    lax.fori_loop(0, HALF // 64, body, 0, unroll=2)
    for copy in copies:
        copy.wait()
    owned = owned_pick(src_ref)
    for g in range(HALF // 512):
        x = raw_ref[:, :, g * 512 : (g + 1) * 512].reshape(2 * CH, 512)
        put_pieces(mine_ref, g, jnp.dot(owned, x, preferred_element_type=F32).astype(BF))
        put_planes(core, g, jnp.dot(planes, x, preferred_element_type=F32))
    day = day_index()
    lane = lax.broadcasted_iota(jnp.int32, (32, LAGS), 1)
    rowi = lax.broadcasted_iota(jnp.int32, (32, LAGS), 0)
    first = jnp.where(rowi < CH, bounds_ref[0, 2 * day], bounds_ref[0, 2 * day + 1])
    last = jnp.where(rowi < CH, bounds_ref[1, 2 * day], bounds_ref[1, 2 * day + 1])
    window_ref[...] = jnp.logical_and(lane >= first, lane < last).astype(F32)
    rows = lax.broadcasted_iota(jnp.int32, (32, LANE), 0) % CH
    cols = lax.broadcasted_iota(jnp.int32, (32, LANE), 1)
    kind = jnp.zeros((32, LANE), jnp.int32)
    for c in range(CH):
        kind = jnp.where(rows == c, intr_ref[c], kind)
    member_ref[0] = (cols == kind).astype(F32)
    member_ref[1] = (cols == kind + NINT).astype(F32)


def other_table_kernel(t_ref, _, o_ref):
    lag = lax.broadcasted_iota(jnp.int32, (2 * 8, LAGS), 1) % 4
    turn = 1.0 - 2.0 * lax.axis_index("core").astype(F32)
    even = jnp.where(lag == 0, 1.0, jnp.where(lag == 2, -1.0, 0.0)).astype(BF)
    odd = (jnp.where(lag == 1, 1.0, jnp.where(lag == 3, -1.0, 0.0)) * turn).astype(BF)

    def body(q, c):
        for r in range(0, CB, 16):
            cos = t_ref[q, r : r + 16, :]
            sin = t_ref[q, CB + r : CB + r + 16, :]
            o_ref[q, r : r + 16, :] = cos * even + sin * odd
            o_ref[q, CB + r : CB + r + 16, :] = sin * even - cos * odd
        return c

    lax.fori_loop(0, CHUNKS // 2, body, 0)


def spread_kernel(p_ref, o_ref):
    n = p_ref.shape[0]
    total = p_ref[0]
    for i in range(1, n):
        total = total + p_ref[i]
    for i in range(n):
        o_ref[i] = total


def build_cross(planes_ref, v_ref, cross_ref, g, off):
    for j in range(CB // LANE):
        lo = pl.multiple_of(off + j * LANE, LANE)
        sr = [planes_ref[8 * i : 8 * i + 8, pl.ds(lo, LANE)] for i in range(2)]
        si = [planes_ref[16 + 8 * i : 24 + 8 * i, pl.ds(lo, LANE)] for i in range(2)]
        for s in range(NSRC):
            vr = v_ref[g * (CB // LANE) + j, pl.ds(s, 8, stride=0), :]
            vi = v_ref[g * (CB // LANE) + j, pl.ds(16 + s, 8, stride=0), :]
            xr = jnp.concatenate([a * vr + b * vi for a, b in zip(sr, si)], 0)
            xi = jnp.concatenate([b * vr - a * vi for a, b in zip(sr, si)], 0)
            row = slice(s * CH, (s + 1) * CH)
            cross_ref[row, j * LANE : (j + 1) * LANE] = xr.astype(BF)
            cross_ref[row, CB + j * LANE : CB + (j + 1) * LANE] = xi.astype(BF)


def half_correlation(planes_ref, v_ref, t_ref, cross_ref, wide_ref, half):
    per_half = CHUNKS // 2
    wide_ref[...] = v_ref[...].astype(F32)
    total = None
    for g in range(per_half):
        build_cross(planes_ref, wide_ref, cross_ref, g, (half * per_half + g) * CB)
        got = jnp.dot(cross_ref[...], t_ref[g], preferred_element_type=F32)
        total = got if total is None else total + got
    return total


def first_half_kernel(planes_ref, v_ref, t_ref, o_ref, cross_ref, wide_ref):
    core = lax.axis_index("core")
    o_ref[...] = half_correlation(planes_ref, v_ref, t_ref, cross_ref, wide_ref, core)


def second_half_kernel(planes_ref, v_ref, t_ref, first_ref, o_ref, cross_ref, wide_ref):
    core = lax.axis_index("core")
    total = half_correlation(planes_ref, v_ref, t_ref, cross_ref, wide_ref, 1 - core)
    o_ref[...] = (first_ref[...] + total).reshape(o_ref.shape)


def drift_kernel(window_ref, member_ref, c_ref, ref_ref, o_ref):
    lane = lax.broadcasted_iota(jnp.int32, (32, LAGS), 1)
    window = window_ref[...] * 0.5
    ahead_w = jnp.where(lane < LAGS - 1, window, 0.0)
    behind_w = jnp.where(lane > 0, window, 0.0)
    in_num = member_ref[0]
    in_den = member_ref[1]
    total = c_ref[0]
    for d in range(1, 8):
        total = total + c_ref[d]
    ref = (total * 0.125).astype(BF)
    ref_ref[...] = ref
    ref = ref.astype(F32)
    for d in range(8):
        corr = c_ref[d]
        slope = pltpu.roll(corr, LAGS - 1, 1) * ahead_w - pltpu.roll(corr, 1, 1) * behind_w
        num = jnp.sum(slope * (corr - ref), axis=1, keepdims=True)
        den = jnp.sum(slope * slope, axis=1, keepdims=True)
        rows = num * in_num + den * in_den
        rows = (rows[0:8] + rows[8:16]) + (rows[16:24] + rows[24:32])
        row = jnp.sum(rows, axis=0, keepdims=True)
        for i in range(4):
            o_ref[d // 4, i, d % 4] = row


def repeat_sum_kernel(p_ref, o_ref):
    total = jnp.sum(jnp.sum(p_ref[...], axis=0), axis=0, keepdims=True)
    for i in range(o_ref.shape[0]):
        o_ref[i] = total


def finish_kernel(p_ref, r_ref, ref_ref, o_ref):
    ref_ref[...] = r_ref[...]
    total = jnp.sum(p_ref[...], axis=0)
    o_ref[...] = total[:, :NINT] / (total[:, NINT : 2 * NINT] + 1e-06)


def call(kernel, out_shape, in_specs, name, scratch=()):
    multi = isinstance(out_shape, (list, tuple))
    return pl.pallas_call(
        kernel,
        out_shape=out_shape,
        in_specs=in_specs,
        out_specs=[VMEM] * len(out_shape) if multi else VMEM,
        scratch_shapes=list(scratch),
        compiler_params=pltpu.CompilerParams(vmem_limit_bytes=16 << 20),
        name=name,
    )


def shaped(shape, dtype):
    return jax.ShapeDtypeStruct(shape, dtype)


PAIR = [(0, 1), (1, 0)]


def per_device(spectra, source_index, interrogator, lag_bounds):
    piece = (16, 32, LANE)
    factors = factor_tables()
    hbm = pl.BlockSpec(memory_space=pltpu.HBM)

    def keep(a):
        return pltpu.with_memory_space_constraint(a, pltpu.HBM)

    spec = keep(spectra.reshape(CH, 2, BINS))
    source_index = keep(source_index)
    half_table = (CHUNKS // 2, 2 * CB, LAGS)
    raw = pltpu.VMEM((CH, 2, HALF), BF)
    other, x, factors = call(
        other_kernel,
        [shaped(piece, BF), shaped((2 * CH, HALF), BF), shaped(factors.shape, F32)],
        [hbm] * 3,
        "other",
        [raw, pltpu.SMEM((NSRC,), jnp.int32), pltpu.SemaphoreType.DMA((3,))],
    )(spec, source_index, keep(jnp.asarray(factors)))
    got = lax.ppermute(other, "core", PAIR)
    mine, table, planes, window, member = call(
        mine_kernel,
        [
            shaped(piece, BF),
            shaped(half_table, BF),
            shaped((32, BINS), F32),
            shaped((32, LAGS), F32),
            shaped((2, 32, LANE), F32),
        ],
        [hbm] * 4 + [VMEM] * 2,
        "mine",
        [
            raw,
            pltpu.SMEM((NSRC,), jnp.int32),
            pltpu.SMEM((CH,), jnp.int32),
            pltpu.SMEM((2, NSRC), jnp.int32),
            pltpu.SemaphoreType.DMA((4,)),
        ],
    )(spec, source_index, keep(interrogator), keep(lag_bounds.T), x, factors)
    parts = lax.all_to_all(mine + got, ("xlo", "z"), 0, 0)
    parts = call(spread_kernel, shaped(piece, BF), [VMEM], "spread")(parts)
    mine_half = lax.all_to_all(parts, ("xlo", "z"), 0, 0)
    other_half = lax.ppermute(mine_half, "core", PAIR)
    crosses = [pltpu.VMEM((NSRC * CH, 2 * CB), BF), pltpu.VMEM(piece, F32)]
    first = call(
        first_half_kernel, shaped((NSRC * CH, LAGS), F32), [VMEM] * 3, "first_half", crosses
    )(planes, mine_half, table)
    other_table = call(
        other_table_kernel,
        shaped(half_table, BF),
        [VMEM, pl.BlockSpec(memory_space=pl.ANY)],
        "other_table",
    )(table, first)
    other_half, other_table = lax.optimization_barrier((other_half, other_table))
    corr = call(
        second_half_kernel, shaped((8, 32, LAGS), F32), [VMEM] * 4, "second_half", crosses
    )(planes, other_half, other_table, first)
    days = lax.all_to_all(corr, ("xhi", "y"), 0, 0)
    ref, fits = call(
        drift_kernel,
        [shaped((32, LAGS), BF), shaped((2, 4, 4, 1, LANE), F32)],
        [VMEM] * 3,
        "drift",
    )(window, member, days)
    fits = lax.all_to_all(fits.reshape(32, 1, LANE), ("xhi", "xlo", "core", "y"), 0, 0)
    fits = call(repeat_sum_kernel, shaped((8, 1, LANE), F32), [VMEM], "near_fits")(fits)
    fits = lax.all_to_all(fits, "z", 0, 0)
    ref, drift = call(
        finish_kernel,
        [shaped((32, LAGS), BF), shaped((1, NINT), F32)],
        [VMEM] * 2,
        "finish",
    )(fits, ref)
    return ref.reshape(2, CH, LAGS), drift


def solution(mesh):
    fine = Mesh(mesh.devices.reshape(8, 2, 2, 2, 4), ("z", "xlo", "core", "xhi", "y"))
    chan = ("z", "xlo", "core")
    day = ("xhi", "y")
    return jax.shard_map(
        per_device,
        mesh=fine,
        in_specs=(P(day, chan, None, None), P(), P(chan), P()),
        out_specs=(P(day, chan, None), P(day, None)),
        check_vma=False,
    )
```

```python
import math

import jax
import jax.numpy as jnp
import numpy as np
from jax import lax
from jax.experimental import pallas as pl
from jax.experimental.pallas import tpu as pltpu
from jax.sharding import Mesh, PartitionSpec as P

LAGS = 256
NINT = 8
BINS = 4096
NSRC = 16
CH = 16
LANE = 128
BF = jnp.bfloat16
F32 = jnp.float32
CHUNKS = 32
CB = BINS // CHUNKS
HALF = BINS // 2
VMEM = pl.BlockSpec(memory_space=pltpu.VMEM)
SMEM = pl.BlockSpec(memory_space=pltpu.SMEM)


def chan_index():
    return (lax.axis_index("z") * 2 + lax.axis_index("xlo")) * 2 + lax.axis_index("core")


def day_index():
    return lax.axis_index("xhi") * 4 + lax.axis_index("y")


def factor_tables():
    tau = np.arange(LAGS, dtype=np.int64)[None, :] - LAGS // 2
    coarse = 64 * np.arange(64, dtype=np.int64)[:, None] * tau
    fine = np.arange(64, dtype=np.int64)[:, None] * tau
    coarse, fine = (math.pi * (f % (2 * BINS)) / BINS for f in (coarse, fine))
    scale = 1.0 / math.sqrt(BINS)
    parts = [np.cos(coarse) * scale, -np.sin(coarse) * scale, np.cos(fine), np.sin(fine)]
    return np.concatenate(parts).astype(np.float32)


def half_range(h):
    return pl.ds(pl.multiple_of(h * HALF, HALF), HALF)


def owned_pick(src_ref):
    base = chan_index() * CH
    rows = lax.broadcasted_iota(jnp.int32, (32, 32), 0)
    cols = lax.broadcasted_iota(jnp.int32, (32, 32), 1)
    want = jnp.full((32, 32), -1, jnp.int32)
    for s in range(NSRC):
        local = src_ref[s] - base
        ok = jnp.logical_and(local >= 0, local < CH)
        first = jnp.where(ok, 2 * local, -1)
        second = jnp.where(ok, 2 * local + 1, -1)
        want = jnp.where(rows == s, first, want)
        want = jnp.where(rows == 16 + s, second, want)
    return (cols == want).astype(F32).astype(BF)


def plane_pick():
    rows = lax.broadcasted_iota(jnp.int32, (32, 32), 0)
    cols = lax.broadcasted_iota(jnp.int32, (32, 32), 1)
    return (cols == 2 * (rows % CH) + rows // CH).astype(F32).astype(BF)


def put_pieces(dst, g, srcs):
    for j in range(4):
        dst[g * 4 + j] = srcs[:, j * LANE : (j + 1) * LANE]


def other_kernel(spec_hbm, src_hbm, f_hbm, other_ref, x_ref, f_ref, raw_ref, src_ref, sems):
    load_src = pltpu.make_async_copy(src_hbm, src_ref, sems.at[0])
    load_src.start()
    part = half_range(1 - lax.axis_index("core"))
    load_x = pltpu.make_async_copy(spec_hbm.at[:, :, part], raw_ref, sems.at[1])
    load_x.start()
    load_f = pltpu.make_async_copy(f_hbm, f_ref, sems.at[2])
    load_f.start()
    load_src.wait()
    pick = owned_pick(src_ref)
    load_x.wait()
    for g in range(HALF // 512):
        at = slice(g * 512, (g + 1) * 512)
        x = raw_ref[:, :, at].reshape(2 * CH, 512)
        x_ref[:, at] = x
        put_pieces(other_ref, g, jnp.dot(pick, x, preferred_element_type=F32).astype(BF))
    load_f.wait()


def mine_kernel(
    spec_hbm,
    src_hbm,
    intr_hbm,
    bounds_hbm,
    x_ref,
    f_ref,
    mine_ref,
    t_ref,
    planes_ref,
    window_ref,
    member_ref,
    raw_ref,
    src_ref,
    intr_ref,
    bounds_ref,
    sems,
):
    core = lax.axis_index("core")
    copies = [
        pltpu.make_async_copy(a, b, sems.at[i])
        for i, (a, b) in enumerate(
            (
                (spec_hbm.at[:, :, half_range(core)], raw_ref),
                (src_hbm, src_ref),
                (intr_hbm, intr_ref),
                (bounds_hbm, bounds_ref),
            )
        )
    ]
    for copy in copies:
        copy.start()
    planes = plane_pick()

    def put_planes(h, g, got):
        off = pl.multiple_of(h * HALF + g * 512, 512)
        planes_ref[:, pl.ds(off, 512)] = got

    for g in range(HALF // 512):
        x = x_ref[:, g * 512 : (g + 1) * 512]
        put_planes(1 - core, g, jnp.dot(planes, x, preferred_element_type=F32))

    def body(a, c):
        ca = f_ref[pl.ds(core * 32 + a, 1), :]
        sa = f_ref[pl.ds(64 + core * 32 + a, 1), :]
        q = a // (CB // 64)
        for i in range(0, 64, 16):
            r = pl.multiple_of((a % (CB // 64)) * 64 + i, 16)
            cb = f_ref[128 + i : 144 + i]
            sb = f_ref[192 + i : 208 + i]
            t_ref[q, pl.ds(r, 16), :] = (ca * cb + sa * sb).astype(BF)
            t_ref[q, pl.ds(CB + r, 16), :] = (sa * cb - ca * sb).astype(BF)
        return c

    lax.fori_loop(0, HALF // 64, body, 0, unroll=2)
    for copy in copies:
        copy.wait()
    owned = owned_pick(src_ref)
    for g in range(HALF // 512):
        x = raw_ref[:, :, g * 512 : (g + 1) * 512].reshape(2 * CH, 512)
        put_pieces(mine_ref, g, jnp.dot(owned, x, preferred_element_type=F32).astype(BF))
        put_planes(core, g, jnp.dot(planes, x, preferred_element_type=F32))
    day = day_index()
    lane = lax.broadcasted_iota(jnp.int32, (32, LAGS), 1)
    rowi = lax.broadcasted_iota(jnp.int32, (32, LAGS), 0)
    first = jnp.where(rowi < CH, bounds_ref[0, 2 * day], bounds_ref[0, 2 * day + 1])
    last = jnp.where(rowi < CH, bounds_ref[1, 2 * day], bounds_ref[1, 2 * day + 1])
    window_ref[...] = jnp.logical_and(lane >= first, lane < last).astype(F32)
    rows = lax.broadcasted_iota(jnp.int32, (32, LANE), 0) % CH
    early = jnp.zeros((32, LANE), F32)
    for c in range(CH):
        same = jnp.where(intr_ref[c] == intr_ref[0], 1.0, 0.0)
        early = jnp.where(rows == c, same, early)
    member_ref[0] = early
    kind = lax.broadcasted_iota(jnp.int32, (8, LANE), 1)
    for i, k in enumerate((intr_ref[0], intr_ref[CH - 1])):
        for j in range(2):
            at = slice(16 * i + 8 * j, 16 * i + 8 * j + 8)
            member_ref[1, at] = (kind == k + NINT * j).astype(F32)


def other_table_kernel(t_ref, _, o_ref):
    lag = lax.broadcasted_iota(jnp.int32, (2 * 8, LAGS), 1) % 4
    turn = 1.0 - 2.0 * lax.axis_index("core").astype(F32)
    even = jnp.where(lag == 0, 1.0, jnp.where(lag == 2, -1.0, 0.0)).astype(BF)
    odd = (jnp.where(lag == 1, 1.0, jnp.where(lag == 3, -1.0, 0.0)) * turn).astype(BF)

    def body(q, c):
        for r in range(0, CB, 16):
            cos = t_ref[q, r : r + 16, :]
            sin = t_ref[q, CB + r : CB + r + 16, :]
            o_ref[q, r : r + 16, :] = cos * even + sin * odd
            o_ref[q, CB + r : CB + r + 16, :] = sin * even - cos * odd
        return c

    lax.fori_loop(0, CHUNKS // 2, body, 0)


def spread_kernel(p_ref, o_ref):
    n = p_ref.shape[0]
    total = p_ref[0]
    for i in range(1, n):
        total = total + p_ref[i]
    for i in range(n):
        o_ref[i] = total


def build_cross(planes_ref, v_ref, cross_ref, g, off):
    for j in range(CB // LANE):
        lo = pl.multiple_of(off + j * LANE, LANE)
        sr = [planes_ref[8 * i : 8 * i + 8, pl.ds(lo, LANE)] for i in range(2)]
        si = [planes_ref[16 + 8 * i : 24 + 8 * i, pl.ds(lo, LANE)] for i in range(2)]
        for s in range(NSRC):
            vr = v_ref[g * (CB // LANE) + j, pl.ds(s, 8, stride=0), :]
            vi = v_ref[g * (CB // LANE) + j, pl.ds(16 + s, 8, stride=0), :]
            xr = jnp.concatenate([a * vr + b * vi for a, b in zip(sr, si)], 0)
            xi = jnp.concatenate([b * vr - a * vi for a, b in zip(sr, si)], 0)
            row = slice(s * CH, (s + 1) * CH)
            cross_ref[row, j * LANE : (j + 1) * LANE] = xr.astype(BF)
            cross_ref[row, CB + j * LANE : CB + (j + 1) * LANE] = xi.astype(BF)


def half_correlation(planes_ref, v_ref, t_ref, cross_ref, wide_ref, half):
    per_half = CHUNKS // 2
    wide_ref[...] = v_ref[...].astype(F32)
    total = None
    for g in range(per_half):
        build_cross(planes_ref, wide_ref, cross_ref, g, (half * per_half + g) * CB)
        got = jnp.dot(cross_ref[...], t_ref[g], preferred_element_type=F32)
        total = got if total is None else total + got
    return total


def first_half_kernel(planes_ref, v_ref, t_ref, o_ref, cross_ref, wide_ref):
    core = lax.axis_index("core")
    o_ref[...] = half_correlation(planes_ref, v_ref, t_ref, cross_ref, wide_ref, core)


def second_half_kernel(planes_ref, v_ref, t_ref, first_ref, o_ref, cross_ref, wide_ref):
    core = lax.axis_index("core")
    total = half_correlation(planes_ref, v_ref, t_ref, cross_ref, wide_ref, 1 - core)
    o_ref[...] = (first_ref[...] + total).reshape(o_ref.shape)


def drift_kernel(window_ref, member_ref, c_ref, ref_ref, o_ref):
    lane = lax.broadcasted_iota(jnp.int32, (32, LAGS), 1)
    window = window_ref[...] * 0.5
    ahead_w = jnp.where(lane < LAGS - 1, window, 0.0)
    behind_w = jnp.where(lane > 0, window, 0.0)
    early = member_ref[0]
    lanes = [member_ref[1, 8 * i : 8 * i + 8] for i in range(4)]

    def fold(x):
        x = x[:, :LANE] + x[:, LANE:]
        parts = []
        for y in (x * early, x - x * early):
            parts.append((y[0:8] + y[8:16]) + (y[16:24] + y[24:32]))
        return [jnp.sum(y, axis=1, keepdims=True) for y in parts]

    total = c_ref[0]
    for d in range(1, 8):
        total = total + c_ref[d]
    ref = (total * 0.125).astype(BF)
    ref_ref[...] = ref
    ref = ref.astype(F32)
    for d in range(8):
        corr = c_ref[d]
        slope = pltpu.roll(corr, LAGS - 1, 1) * ahead_w - pltpu.roll(corr, 1, 1) * behind_w
        num = fold(slope * (corr - ref))
        den = fold(slope * slope)
        rows = (num[0] * lanes[0] + den[0] * lanes[1]) + (num[1] * lanes[2] + den[1] * lanes[3])
        row = jnp.sum(rows, axis=0, keepdims=True)
        for i in range(4):
            o_ref[d // 4, i, d % 4] = row


def repeat_sum_kernel(p_ref, o_ref):
    total = jnp.sum(jnp.sum(p_ref[...], axis=0), axis=0, keepdims=True)
    for i in range(o_ref.shape[0]):
        o_ref[i] = total


def finish_kernel(p_ref, r_ref, ref_ref, o_ref):
    ref_ref[...] = r_ref[...]
    total = jnp.sum(p_ref[...], axis=0)
    o_ref[...] = total[:, :NINT] / (total[:, NINT : 2 * NINT] + 1e-06)


def call(kernel, out_shape, in_specs, name, scratch=()):
    multi = isinstance(out_shape, (list, tuple))
    return pl.pallas_call(
        kernel,
        out_shape=out_shape,
        in_specs=in_specs,
        out_specs=[VMEM] * len(out_shape) if multi else VMEM,
        scratch_shapes=list(scratch),
        compiler_params=pltpu.CompilerParams(vmem_limit_bytes=16 << 20),
        name=name,
    )


def shaped(shape, dtype):
    return jax.ShapeDtypeStruct(shape, dtype)


PAIR = [(0, 1), (1, 0)]


def per_device(spectra, source_index, interrogator, lag_bounds):
    piece = (16, 32, LANE)
    factors = factor_tables()
    hbm = pl.BlockSpec(memory_space=pltpu.HBM)

    def keep(a):
        return pltpu.with_memory_space_constraint(a, pltpu.HBM)

    spec = keep(spectra.reshape(CH, 2, BINS))
    source_index = keep(source_index)
    half_table = (CHUNKS // 2, 2 * CB, LAGS)
    raw = pltpu.VMEM((CH, 2, HALF), BF)
    other, x, factors = call(
        other_kernel,
        [shaped(piece, BF), shaped((2 * CH, HALF), BF), shaped(factors.shape, F32)],
        [hbm] * 3,
        "other",
        [raw, pltpu.SMEM((NSRC,), jnp.int32), pltpu.SemaphoreType.DMA((3,))],
    )(spec, source_index, keep(jnp.asarray(factors)))
    got = lax.ppermute(other, "core", PAIR)
    mine, table, planes, window, member = call(
        mine_kernel,
        [
            shaped(piece, BF),
            shaped(half_table, BF),
            shaped((32, BINS), F32),
            shaped((32, LAGS), F32),
            shaped((2, 32, LANE), F32),
        ],
        [hbm] * 4 + [VMEM] * 2,
        "mine",
        [
            raw,
            pltpu.SMEM((NSRC,), jnp.int32),
            pltpu.SMEM((CH,), jnp.int32),
            pltpu.SMEM((2, NSRC), jnp.int32),
            pltpu.SemaphoreType.DMA((4,)),
        ],
    )(spec, source_index, keep(interrogator), keep(lag_bounds.T), x, factors)
    parts = lax.all_to_all(mine + got, ("xlo", "z"), 0, 0)
    parts = call(spread_kernel, shaped(piece, BF), [VMEM], "spread")(parts)
    mine_half = lax.all_to_all(parts, ("xlo", "z"), 0, 0)
    other_half = lax.ppermute(mine_half, "core", PAIR)
    crosses = [pltpu.VMEM((NSRC * CH, 2 * CB), BF), pltpu.VMEM(piece, F32)]
    first = call(
        first_half_kernel, shaped((NSRC * CH, LAGS), F32), [VMEM] * 3, "first_half", crosses
    )(planes, mine_half, table)
    other_table = call(
        other_table_kernel,
        shaped(half_table, BF),
        [VMEM, pl.BlockSpec(memory_space=pl.ANY)],
        "other_table",
    )(table, first)
    other_half, other_table = lax.optimization_barrier((other_half, other_table))
    corr = call(
        second_half_kernel, shaped((8, 32, LAGS), F32), [VMEM] * 4, "second_half", crosses
    )(planes, other_half, other_table, first)
    days = lax.all_to_all(corr, ("xhi", "y"), 0, 0)
    ref, fits = call(
        drift_kernel,
        [shaped((32, LAGS), BF), shaped((2, 4, 4, 1, LANE), F32)],
        [VMEM] * 3,
        "drift",
    )(window, member, days)
    fits = lax.all_to_all(fits.reshape(32, 1, LANE), ("xhi", "xlo", "core", "y"), 0, 0)
    fits = call(repeat_sum_kernel, shaped((8, 1, LANE), F32), [VMEM], "near_fits")(fits)
    fits = lax.all_to_all(fits, "z", 0, 0)
    ref, drift = call(
        finish_kernel,
        [shaped((32, LAGS), BF), shaped((1, NINT), F32)],
        [VMEM] * 2,
        "finish",
    )(fits, ref)
    return ref.reshape(2, CH, LAGS), drift


def solution(mesh):
    fine = Mesh(mesh.devices.reshape(8, 2, 2, 2, 4), ("z", "xlo", "core", "xhi", "y"))
    chan = ("z", "xlo", "core")
    day = ("xhi", "y")
    return jax.shard_map(
        per_device,
        mesh=fine,
        in_specs=(P(day, chan, None, None), P(), P(chan), P()),
        out_specs=(P(day, chan, None), P(day, None)),
        check_vma=False,
    )
```

```python
import math

import jax
import jax.numpy as jnp
import numpy as np
from jax import lax
from jax.experimental import pallas as pl
from jax.experimental.pallas import tpu as pltpu
from jax.sharding import Mesh, PartitionSpec as P

LAGS = 256
NINT = 8
BINS = 4096
NSRC = 16
CH = 16
LANE = 128
BF = jnp.bfloat16
F32 = jnp.float32
CHUNKS = 32
CB = BINS // CHUNKS
HALF = BINS // 2
VMEM = pl.BlockSpec(memory_space=pltpu.VMEM)
SMEM = pl.BlockSpec(memory_space=pltpu.SMEM)


def chan_index():
    return (lax.axis_index("z") * 2 + lax.axis_index("xlo")) * 2 + lax.axis_index("core")


def day_index():
    return lax.axis_index("xhi") * 4 + lax.axis_index("y")


def factor_tables():
    tau = np.arange(LAGS, dtype=np.int64)[None, :] - LAGS // 2
    coarse = 64 * np.arange(64, dtype=np.int64)[:, None] * tau
    fine = np.arange(64, dtype=np.int64)[:, None] * tau
    coarse, fine = (math.pi * (f % (2 * BINS)) / BINS for f in (coarse, fine))
    scale = 1.0 / math.sqrt(BINS)
    parts = [np.cos(coarse) * scale, -np.sin(coarse) * scale, np.cos(fine), np.sin(fine)]
    own = [p[h : h + 32] for h in (0, 32) for p in parts[:2]]
    return np.concatenate(own + parts[2:]).astype(np.float32)


def half_range(h):
    return pl.ds(pl.multiple_of(h * HALF, HALF), HALF)


def owned_pick(src_ref):
    base = chan_index() * CH
    rows = lax.broadcasted_iota(jnp.int32, (32, 32), 0)
    cols = lax.broadcasted_iota(jnp.int32, (32, 32), 1)
    want = jnp.full((32, 32), -1, jnp.int32)
    for s in range(NSRC):
        local = src_ref[s] - base
        ok = jnp.logical_and(local >= 0, local < CH)
        first = jnp.where(ok, 2 * local, -1)
        second = jnp.where(ok, 2 * local + 1, -1)
        want = jnp.where(rows == s, first, want)
        want = jnp.where(rows == 16 + s, second, want)
    return (cols == want).astype(F32).astype(BF)


def plane_pick():
    rows = lax.broadcasted_iota(jnp.int32, (32, 32), 0)
    cols = lax.broadcasted_iota(jnp.int32, (32, 32), 1)
    return (cols == 2 * (rows % CH) + rows // CH).astype(F32).astype(BF)


def put_pieces(dst, g, srcs):
    for j in range(4):
        dst[g * 4 + j] = srcs[:, j * LANE : (j + 1) * LANE]


def other_kernel(spec_hbm, src_hbm, f_hbm, other_ref, x_ref, f_ref, raw_ref, src_ref, sems):
    load_src = pltpu.make_async_copy(src_hbm, src_ref, sems.at[0])
    load_src.start()
    part = half_range(1 - lax.axis_index("core"))
    load_x = pltpu.make_async_copy(spec_hbm.at[:, :, part], raw_ref, sems.at[1])
    load_x.start()
    own = pl.ds(pl.multiple_of(lax.axis_index("core") * 64, 64), 64)
    loads_f = [
        pltpu.make_async_copy(f_hbm.at[own], f_ref.at[0:64], sems.at[2]),
        pltpu.make_async_copy(f_hbm.at[128:256], f_ref.at[64:192], sems.at[3]),
    ]
    for load in loads_f:
        load.start()
    load_src.wait()
    pick = owned_pick(src_ref)
    load_x.wait()
    for g in range(HALF // 512):
        at = slice(g * 512, (g + 1) * 512)
        x = raw_ref[:, :, at].reshape(2 * CH, 512)
        x_ref[:, at] = x
        put_pieces(other_ref, g, jnp.dot(pick, x, preferred_element_type=F32).astype(BF))
    for load in loads_f:
        load.wait()


def mine_kernel(
    spec_hbm,
    src_hbm,
    intr_hbm,
    bounds_hbm,
    x_ref,
    f_ref,
    mine_ref,
    t_ref,
    planes_ref,
    window_ref,
    member_ref,
    raw_ref,
    src_ref,
    intr_ref,
    bounds_ref,
    sems,
):
    core = lax.axis_index("core")
    copies = [
        pltpu.make_async_copy(a, b, sems.at[i])
        for i, (a, b) in enumerate(
            (
                (spec_hbm.at[:, :, half_range(core)], raw_ref),
                (src_hbm, src_ref),
                (intr_hbm, intr_ref),
                (bounds_hbm, bounds_ref),
            )
        )
    ]
    for copy in copies:
        copy.start()
    planes = plane_pick()

    def put_planes(h, g, got):
        off = pl.multiple_of(h * HALF + g * 512, 512)
        planes_ref[:, pl.ds(off, 512)] = got

    for g in range(HALF // 512):
        x = x_ref[:, g * 512 : (g + 1) * 512]
        put_planes(1 - core, g, jnp.dot(planes, x, preferred_element_type=F32))

    def body(a, c):
        ca = f_ref[pl.ds(a, 1), :]
        sa = f_ref[pl.ds(32 + a, 1), :]
        q = a // (CB // 64)
        for i in range(0, 64, 16):
            r = pl.multiple_of((a % (CB // 64)) * 64 + i, 16)
            cb = f_ref[64 + i : 80 + i]
            sb = f_ref[128 + i : 144 + i]
            t_ref[q, pl.ds(r, 16), :] = (ca * cb + sa * sb).astype(BF)
            t_ref[q, pl.ds(CB + r, 16), :] = (sa * cb - ca * sb).astype(BF)
        return c

    lax.fori_loop(0, HALF // 64, body, 0, unroll=2)
    for copy in copies:
        copy.wait()
    owned = owned_pick(src_ref)
    for g in range(HALF // 512):
        x = raw_ref[:, :, g * 512 : (g + 1) * 512].reshape(2 * CH, 512)
        put_pieces(mine_ref, g, jnp.dot(owned, x, preferred_element_type=F32).astype(BF))
        put_planes(core, g, jnp.dot(planes, x, preferred_element_type=F32))
    day = day_index()
    lane = lax.broadcasted_iota(jnp.int32, (32, LAGS), 1)
    rowi = lax.broadcasted_iota(jnp.int32, (32, LAGS), 0)
    first = jnp.where(rowi < CH, bounds_ref[0, 2 * day], bounds_ref[0, 2 * day + 1])
    last = jnp.where(rowi < CH, bounds_ref[1, 2 * day], bounds_ref[1, 2 * day + 1])
    window_ref[...] = jnp.logical_and(lane >= first, lane < last).astype(F32)
    rows = lax.broadcasted_iota(jnp.int32, (32, LANE), 0) % CH
    early = jnp.zeros((32, LANE), F32)
    for c in range(CH):
        same = jnp.where(intr_ref[c] == intr_ref[0], 1.0, 0.0)
        early = jnp.where(rows == c, same, early)
    member_ref[0] = early
    kind = lax.broadcasted_iota(jnp.int32, (8, LANE), 1)
    for i, k in enumerate((intr_ref[0], intr_ref[CH - 1])):
        for j in range(2):
            at = slice(16 * i + 8 * j, 16 * i + 8 * j + 8)
            member_ref[1, at] = (kind == k + NINT * j).astype(F32)


def other_table_kernel(t_ref, _, o_ref):
    lag = lax.broadcasted_iota(jnp.int32, (2 * 8, LAGS), 1) % 4
    turn = 1.0 - 2.0 * lax.axis_index("core").astype(F32)
    even = jnp.where(lag == 0, 1.0, jnp.where(lag == 2, -1.0, 0.0)).astype(BF)
    odd = (jnp.where(lag == 1, 1.0, jnp.where(lag == 3, -1.0, 0.0)) * turn).astype(BF)

    def body(q, c):
        for r in range(0, CB, 16):
            cos = t_ref[q, r : r + 16, :]
            sin = t_ref[q, CB + r : CB + r + 16, :]
            o_ref[q, r : r + 16, :] = cos * even + sin * odd
            o_ref[q, CB + r : CB + r + 16, :] = sin * even - cos * odd
        return c

    lax.fori_loop(0, CHUNKS // 2, body, 0)


def spread_kernel(p_ref, o_ref):
    n = p_ref.shape[0]
    total = p_ref[0]
    for i in range(1, n):
        total = total + p_ref[i]
    for i in range(n):
        o_ref[i] = total


def build_cross(planes_ref, v_ref, cross_ref, g, off):
    for j in range(CB // LANE):
        lo = pl.multiple_of(off + j * LANE, LANE)
        sr = [planes_ref[8 * i : 8 * i + 8, pl.ds(lo, LANE)] for i in range(2)]
        si = [planes_ref[16 + 8 * i : 24 + 8 * i, pl.ds(lo, LANE)] for i in range(2)]
        for s in range(NSRC):
            vr = v_ref[g * (CB // LANE) + j, pl.ds(s, 8, stride=0), :]
            vi = v_ref[g * (CB // LANE) + j, pl.ds(16 + s, 8, stride=0), :]
            xr = jnp.concatenate([a * vr + b * vi for a, b in zip(sr, si)], 0)
            xi = jnp.concatenate([b * vr - a * vi for a, b in zip(sr, si)], 0)
            row = slice(s * CH, (s + 1) * CH)
            cross_ref[row, j * LANE : (j + 1) * LANE] = xr.astype(BF)
            cross_ref[row, CB + j * LANE : CB + (j + 1) * LANE] = xi.astype(BF)


def half_correlation(planes_ref, v_ref, t_ref, cross_ref, wide_ref, half):
    per_half = CHUNKS // 2
    wide_ref[...] = v_ref[...].astype(F32)
    total = None
    for g in range(per_half):
        build_cross(planes_ref, wide_ref, cross_ref, g, (half * per_half + g) * CB)
        got = jnp.dot(cross_ref[...], t_ref[g], preferred_element_type=F32)
        total = got if total is None else total + got
    return total


def first_half_kernel(planes_ref, v_ref, t_ref, o_ref, cross_ref, wide_ref):
    core = lax.axis_index("core")
    o_ref[...] = half_correlation(planes_ref, v_ref, t_ref, cross_ref, wide_ref, core)


def second_half_kernel(planes_ref, v_ref, t_ref, first_ref, o_ref, cross_ref, wide_ref):
    core = lax.axis_index("core")
    total = half_correlation(planes_ref, v_ref, t_ref, cross_ref, wide_ref, 1 - core)
    o_ref[...] = (first_ref[...] + total).reshape(o_ref.shape)


def drift_kernel(window_ref, member_ref, c_ref, ref_ref, o_ref):
    lane = lax.broadcasted_iota(jnp.int32, (32, LAGS), 1)
    window = window_ref[...] * 0.5
    ahead_w = jnp.where(lane < LAGS - 1, window, 0.0)
    behind_w = jnp.where(lane > 0, window, 0.0)
    early = member_ref[0]
    lanes = [member_ref[1, 8 * i : 8 * i + 8] for i in range(4)]

    def fold(x):
        x = x[:, :LANE] + x[:, LANE:]
        parts = []
        for y in (x * early, x - x * early):
            parts.append((y[0:8] + y[8:16]) + (y[16:24] + y[24:32]))
        return [jnp.sum(y, axis=1, keepdims=True) for y in parts]

    total = c_ref[0]
    for d in range(1, 8):
        total = total + c_ref[d]
    ref = (total * 0.125).astype(BF)
    ref_ref[...] = ref
    ref = ref.astype(F32)
    for d in range(8):
        corr = c_ref[d]
        slope = pltpu.roll(corr, LAGS - 1, 1) * ahead_w - pltpu.roll(corr, 1, 1) * behind_w
        num = fold(slope * (corr - ref))
        den = fold(slope * slope)
        rows = (num[0] * lanes[0] + den[0] * lanes[1]) + (num[1] * lanes[2] + den[1] * lanes[3])
        row = jnp.sum(rows, axis=0, keepdims=True)
        for i in range(4):
            o_ref[d // 4, i, d % 4] = row


def repeat_sum_kernel(p_ref, o_ref):
    total = jnp.sum(jnp.sum(p_ref[...], axis=0), axis=0, keepdims=True)
    for i in range(o_ref.shape[0]):
        o_ref[i] = total


def finish_kernel(p_ref, r_ref, ref_ref, o_ref):
    ref_ref[...] = r_ref[...]
    total = jnp.sum(p_ref[...], axis=0)
    o_ref[...] = total[:, :NINT] / (total[:, NINT : 2 * NINT] + 1e-06)


def call(kernel, out_shape, in_specs, name, scratch=()):
    multi = isinstance(out_shape, (list, tuple))
    return pl.pallas_call(
        kernel,
        out_shape=out_shape,
        in_specs=in_specs,
        out_specs=[VMEM] * len(out_shape) if multi else VMEM,
        scratch_shapes=list(scratch),
        compiler_params=pltpu.CompilerParams(vmem_limit_bytes=16 << 20),
        name=name,
    )


def shaped(shape, dtype):
    return jax.ShapeDtypeStruct(shape, dtype)


PAIR = [(0, 1), (1, 0)]


def per_device(spectra, source_index, interrogator, lag_bounds):
    piece = (16, 32, LANE)
    factors = factor_tables()
    hbm = pl.BlockSpec(memory_space=pltpu.HBM)

    def keep(a):
        return pltpu.with_memory_space_constraint(a, pltpu.HBM)

    spec = keep(spectra.reshape(CH, 2, BINS))
    source_index = keep(source_index)
    half_table = (CHUNKS // 2, 2 * CB, LAGS)
    raw = pltpu.VMEM((CH, 2, HALF), BF)
    other, x, factors = call(
        other_kernel,
        [shaped(piece, BF), shaped((2 * CH, HALF), BF), shaped((192, LAGS), F32)],
        [hbm] * 3,
        "other",
        [raw, pltpu.SMEM((NSRC,), jnp.int32), pltpu.SemaphoreType.DMA((4,))],
    )(spec, source_index, keep(jnp.asarray(factors)))
    got = lax.ppermute(other, "core", PAIR)
    mine, table, planes, window, member = call(
        mine_kernel,
        [
            shaped(piece, BF),
            shaped(half_table, BF),
            shaped((32, BINS), F32),
            shaped((32, LAGS), F32),
            shaped((2, 32, LANE), F32),
        ],
        [hbm] * 4 + [VMEM] * 2,
        "mine",
        [
            raw,
            pltpu.SMEM((NSRC,), jnp.int32),
            pltpu.SMEM((CH,), jnp.int32),
            pltpu.SMEM((2, NSRC), jnp.int32),
            pltpu.SemaphoreType.DMA((4,)),
        ],
    )(spec, source_index, keep(interrogator), keep(lag_bounds.T), x, factors)
    parts = lax.all_to_all(mine + got, ("xlo", "z"), 0, 0)
    parts = call(spread_kernel, shaped(piece, BF), [VMEM], "spread")(parts)
    mine_half = lax.all_to_all(parts, ("xlo", "z"), 0, 0)
    other_half = lax.ppermute(mine_half, "core", PAIR)
    crosses = [pltpu.VMEM((NSRC * CH, 2 * CB), BF), pltpu.VMEM(piece, F32)]
    first = call(
        first_half_kernel, shaped((NSRC * CH, LAGS), F32), [VMEM] * 3, "first_half", crosses
    )(planes, mine_half, table)
    other_table = call(
        other_table_kernel,
        shaped(half_table, BF),
        [VMEM, pl.BlockSpec(memory_space=pl.ANY)],
        "other_table",
    )(table, first)
    other_half, other_table = lax.optimization_barrier((other_half, other_table))
    corr = call(
        second_half_kernel, shaped((8, 32, LAGS), F32), [VMEM] * 4, "second_half", crosses
    )(planes, other_half, other_table, first)
    days = lax.all_to_all(corr, ("xhi", "y"), 0, 0)
    ref, fits = call(
        drift_kernel,
        [shaped((32, LAGS), BF), shaped((2, 4, 4, 1, LANE), F32)],
        [VMEM] * 3,
        "drift",
    )(window, member, days)
    fits = lax.all_to_all(fits.reshape(32, 1, LANE), ("xhi", "xlo", "core", "y"), 0, 0)
    fits = call(repeat_sum_kernel, shaped((8, 1, LANE), F32), [VMEM], "near_fits")(fits)
    fits = lax.all_to_all(fits, "z", 0, 0)
    ref, drift = call(
        finish_kernel,
        [shaped((32, LAGS), BF), shaped((1, NINT), F32)],
        [VMEM] * 2,
        "finish",
    )(fits, ref)
    return ref.reshape(2, CH, LAGS), drift


def solution(mesh):
    fine = Mesh(mesh.devices.reshape(8, 2, 2, 2, 4), ("z", "xlo", "core", "xhi", "y"))
    chan = ("z", "xlo", "core")
    day = ("xhi", "y")
    return jax.shard_map(
        per_device,
        mesh=fine,
        in_specs=(P(day, chan, None, None), P(), P(chan), P()),
        out_specs=(P(day, chan, None), P(day, None)),
        check_vma=False,
    )
```

```python
import math

import jax
import jax.numpy as jnp
import numpy as np
from jax import lax
from jax.experimental import pallas as pl
from jax.experimental.pallas import tpu as pltpu
from jax.sharding import Mesh, PartitionSpec as P

LAGS = 256
NINT = 8
BINS = 4096
NSRC = 16
CH = 16
LANE = 128
BF = jnp.bfloat16
F32 = jnp.float32
CHUNKS = 32
CB = BINS // CHUNKS
HALF = BINS // 2
VMEM = pl.BlockSpec(memory_space=pltpu.VMEM)
SMEM = pl.BlockSpec(memory_space=pltpu.SMEM)


def chan_index():
    return (lax.axis_index("z") * 2 + lax.axis_index("xlo")) * 2 + lax.axis_index("core")


def day_index():
    return lax.axis_index("xhi") * 4 + lax.axis_index("y")


def factor_tables():
    tau = np.arange(LAGS, dtype=np.int64)[None, :] - LAGS // 2
    coarse = 64 * np.arange(64, dtype=np.int64)[:, None] * tau
    fine = np.arange(64, dtype=np.int64)[:, None] * tau
    coarse, fine = (math.pi * (f % (2 * BINS)) / BINS for f in (coarse, fine))
    scale = 1.0 / math.sqrt(BINS)
    parts = [np.cos(coarse) * scale, -np.sin(coarse) * scale, np.cos(fine), np.sin(fine)]
    own = [p[h : h + 32] for h in (0, 32) for p in parts[:2]]
    return np.concatenate(own + parts[2:]).astype(np.float32)


def half_range(h):
    return pl.ds(pl.multiple_of(h * HALF, HALF), HALF)


def owned_pick(src_ref):
    base = chan_index() * CH
    rows = lax.broadcasted_iota(jnp.int32, (32, 32), 0)
    cols = lax.broadcasted_iota(jnp.int32, (32, 32), 1)
    want = jnp.full((32, 32), -1, jnp.int32)
    for s in range(NSRC):
        local = src_ref[s] - base
        ok = jnp.logical_and(local >= 0, local < CH)
        first = jnp.where(ok, 2 * local, -1)
        second = jnp.where(ok, 2 * local + 1, -1)
        want = jnp.where(rows == s, first, want)
        want = jnp.where(rows == 16 + s, second, want)
    return (cols == want).astype(F32).astype(BF)


def plane_pick():
    rows = lax.broadcasted_iota(jnp.int32, (32, 32), 0)
    cols = lax.broadcasted_iota(jnp.int32, (32, 32), 1)
    return (cols == 2 * (rows % CH) + rows // CH).astype(F32).astype(BF)


def put_pieces(dst, g, srcs):
    for j in range(4):
        dst[g * 4 + j] = srcs[:, j * LANE : (j + 1) * LANE]


def other_kernel(spec_hbm, src_hbm, f_hbm, other_ref, x_ref, f_ref, raw_ref, src_ref, sems):
    load_src = pltpu.make_async_copy(src_hbm, src_ref, sems.at[0])
    load_src.start()
    part = half_range(1 - lax.axis_index("core"))
    load_x = pltpu.make_async_copy(spec_hbm.at[:, :, part], raw_ref, sems.at[1])
    load_x.start()
    own = pl.ds(pl.multiple_of(lax.axis_index("core") * 64, 64), 64)
    loads_f = [
        pltpu.make_async_copy(f_hbm.at[own], f_ref.at[0:64], sems.at[2]),
        pltpu.make_async_copy(f_hbm.at[128:256], f_ref.at[64:192], sems.at[3]),
    ]
    for load in loads_f:
        load.start()
    load_src.wait()
    pick = owned_pick(src_ref)
    load_x.wait()
    for g in range(HALF // 512):
        at = slice(g * 512, (g + 1) * 512)
        x = raw_ref[:, :, at].reshape(2 * CH, 512)
        x_ref[:, at] = x
        put_pieces(other_ref, g, jnp.dot(pick, x, preferred_element_type=F32).astype(BF))
    for load in loads_f:
        load.wait()


def mine_kernel(
    spec_hbm,
    src_hbm,
    intr_hbm,
    bounds_hbm,
    x_ref,
    f_ref,
    mine_ref,
    t_ref,
    planes_ref,
    window_ref,
    member_ref,
    raw_ref,
    src_ref,
    intr_ref,
    bounds_ref,
    sems,
):
    core = lax.axis_index("core")
    copies = [
        pltpu.make_async_copy(a, b, sems.at[i])
        for i, (a, b) in enumerate(
            (
                (spec_hbm.at[:, :, half_range(core)], raw_ref),
                (src_hbm, src_ref),
                (intr_hbm, intr_ref),
                (bounds_hbm, bounds_ref),
            )
        )
    ]
    for copy in copies:
        copy.start()
    planes = plane_pick()

    def put_planes(h, g, got):
        off = pl.multiple_of(h * HALF + g * 512, 512)
        planes_ref[:, pl.ds(off, 512)] = got

    for g in range(HALF // 512):
        x = x_ref[:, g * 512 : (g + 1) * 512]
        put_planes(1 - core, g, jnp.dot(planes, x, preferred_element_type=F32))

    def body(a, c):
        ca = f_ref[pl.ds(a, 1), :]
        sa = f_ref[pl.ds(32 + a, 1), :]
        q = a // (CB // 64)
        for i in range(0, 64, 16):
            r = pl.multiple_of((a % (CB // 64)) * 64 + i, 16)
            cb = f_ref[64 + i : 80 + i]
            sb = f_ref[128 + i : 144 + i]
            t_ref[q, pl.ds(r, 16), :] = (ca * cb + sa * sb).astype(BF)
            t_ref[q, pl.ds(CB + r, 16), :] = (sa * cb - ca * sb).astype(BF)
        return c

    lax.fori_loop(0, HALF // 64, body, 0, unroll=2)
    for copy in copies:
        copy.wait()
    owned = owned_pick(src_ref)
    for g in range(HALF // 512):
        x = raw_ref[:, :, g * 512 : (g + 1) * 512].reshape(2 * CH, 512)
        put_pieces(mine_ref, g, jnp.dot(owned, x, preferred_element_type=F32).astype(BF))
        put_planes(core, g, jnp.dot(planes, x, preferred_element_type=F32))
    day = day_index()
    lane = lax.broadcasted_iota(jnp.int32, (32, LAGS), 1)
    rowi = lax.broadcasted_iota(jnp.int32, (32, LAGS), 0)
    first = jnp.where(rowi < CH, bounds_ref[0, 2 * day], bounds_ref[0, 2 * day + 1])
    last = jnp.where(rowi < CH, bounds_ref[1, 2 * day], bounds_ref[1, 2 * day + 1])
    window_ref[...] = jnp.logical_and(lane >= first, lane < last).astype(F32)
    rows = lax.broadcasted_iota(jnp.int32, (32, LANE), 0) % CH
    early = jnp.zeros((32, LANE), F32)
    for c in range(CH):
        same = jnp.where(intr_ref[c] == intr_ref[0], 1.0, 0.0)
        early = jnp.where(rows == c, same, early)
    member_ref[0] = early
    kind = lax.broadcasted_iota(jnp.int32, (8, LANE), 1)
    for i, k in enumerate((intr_ref[0], intr_ref[CH - 1])):
        for j in range(2):
            at = slice(16 * i + 8 * j, 16 * i + 8 * j + 8)
            member_ref[1, at] = (kind == k + NINT * j).astype(F32)


def other_table_kernel(t_ref, _, o_ref):
    lag = lax.broadcasted_iota(jnp.int32, (2 * 8, LAGS), 1) % 4
    turn = 1.0 - 2.0 * lax.axis_index("core").astype(F32)
    even = jnp.where(lag == 0, 1.0, jnp.where(lag == 2, -1.0, 0.0)).astype(BF)
    odd = (jnp.where(lag == 1, 1.0, jnp.where(lag == 3, -1.0, 0.0)) * turn).astype(BF)

    def body(q, c):
        for r in range(0, CB, 16):
            cos = t_ref[q, r : r + 16, :]
            sin = t_ref[q, CB + r : CB + r + 16, :]
            o_ref[q, r : r + 16, :] = cos * even + sin * odd
            o_ref[q, CB + r : CB + r + 16, :] = sin * even - cos * odd
        return c

    lax.fori_loop(0, CHUNKS // 2, body, 0, unroll=2)


def spread_kernel(p_ref, o_ref):
    n = p_ref.shape[0]
    total = p_ref[0]
    for i in range(1, n):
        total = total + p_ref[i]
    for i in range(n):
        o_ref[i] = total


def build_cross(planes_ref, v_ref, cross_ref, g, off):
    for j in range(CB // LANE):
        lo = pl.multiple_of(off + j * LANE, LANE)
        sr = [planes_ref[8 * i : 8 * i + 8, pl.ds(lo, LANE)] for i in range(2)]
        si = [planes_ref[16 + 8 * i : 24 + 8 * i, pl.ds(lo, LANE)] for i in range(2)]
        for s in range(NSRC):
            vr = v_ref[g * (CB // LANE) + j, pl.ds(s, 8, stride=0), :]
            vi = v_ref[g * (CB // LANE) + j, pl.ds(16 + s, 8, stride=0), :]
            xr = jnp.concatenate([a * vr + b * vi for a, b in zip(sr, si)], 0)
            xi = jnp.concatenate([b * vr - a * vi for a, b in zip(sr, si)], 0)
            row = slice(s * CH, (s + 1) * CH)
            cross_ref[row, j * LANE : (j + 1) * LANE] = xr.astype(BF)
            cross_ref[row, CB + j * LANE : CB + (j + 1) * LANE] = xi.astype(BF)


def half_correlation(planes_ref, v_ref, t_ref, cross_ref, wide_ref, half):
    per_half = CHUNKS // 2
    wide_ref[...] = v_ref[...].astype(F32)
    total = None
    for g in range(per_half):
        build_cross(planes_ref, wide_ref, cross_ref, g, (half * per_half + g) * CB)
        got = jnp.dot(cross_ref[...], t_ref[g], preferred_element_type=F32)
        total = got if total is None else total + got
    return total


def first_half_kernel(planes_ref, v_ref, t_ref, o_ref, cross_ref, wide_ref):
    core = lax.axis_index("core")
    o_ref[...] = half_correlation(planes_ref, v_ref, t_ref, cross_ref, wide_ref, core)


def second_half_kernel(planes_ref, v_ref, t_ref, first_ref, o_ref, cross_ref, wide_ref):
    core = lax.axis_index("core")
    total = half_correlation(planes_ref, v_ref, t_ref, cross_ref, wide_ref, 1 - core)
    o_ref[...] = (first_ref[...] + total).reshape(o_ref.shape)


def drift_kernel(window_ref, member_ref, c_ref, ref_ref, o_ref):
    lane = lax.broadcasted_iota(jnp.int32, (32, LAGS), 1)
    window = window_ref[...] * 0.5
    ahead_w = jnp.where(lane < LAGS - 1, window, 0.0)
    behind_w = jnp.where(lane > 0, window, 0.0)
    early = member_ref[0]
    lanes = [member_ref[1, 8 * i : 8 * i + 8] for i in range(4)]

    def fold(x):
        x = x[:, :LANE] + x[:, LANE:]
        parts = []
        for y in (x * early, x - x * early):
            parts.append((y[0:8] + y[8:16]) + (y[16:24] + y[24:32]))
        return [jnp.sum(y, axis=1, keepdims=True) for y in parts]

    total = c_ref[0]
    for d in range(1, 8):
        total = total + c_ref[d]
    ref = (total * 0.125).astype(BF)
    ref_ref[...] = ref
    ref = ref.astype(F32)
    for d in range(8):
        corr = c_ref[d]
        slope = pltpu.roll(corr, LAGS - 1, 1) * ahead_w - pltpu.roll(corr, 1, 1) * behind_w
        num = fold(slope * (corr - ref))
        den = fold(slope * slope)
        rows = (num[0] * lanes[0] + den[0] * lanes[1]) + (num[1] * lanes[2] + den[1] * lanes[3])
        row = jnp.sum(rows, axis=0, keepdims=True)
        for i in range(4):
            o_ref[d // 4, i, d % 4] = row


def repeat_sum_kernel(p_ref, o_ref):
    total = jnp.sum(jnp.sum(p_ref[...], axis=0), axis=0, keepdims=True)
    for i in range(o_ref.shape[0]):
        o_ref[i] = total


def finish_kernel(p_ref, r_ref, ref_ref, o_ref):
    ref_ref[...] = r_ref[...]
    total = jnp.sum(p_ref[...], axis=0)
    o_ref[...] = total[:, :NINT] / (total[:, NINT : 2 * NINT] + 1e-06)


def call(kernel, out_shape, in_specs, name, scratch=()):
    multi = isinstance(out_shape, (list, tuple))
    return pl.pallas_call(
        kernel,
        out_shape=out_shape,
        in_specs=in_specs,
        out_specs=[VMEM] * len(out_shape) if multi else VMEM,
        scratch_shapes=list(scratch),
        compiler_params=pltpu.CompilerParams(vmem_limit_bytes=16 << 20),
        name=name,
    )


def shaped(shape, dtype):
    return jax.ShapeDtypeStruct(shape, dtype)


PAIR = [(0, 1), (1, 0)]


def per_device(spectra, source_index, interrogator, lag_bounds):
    piece = (16, 32, LANE)
    factors = factor_tables()
    hbm = pl.BlockSpec(memory_space=pltpu.HBM)

    def keep(a):
        return pltpu.with_memory_space_constraint(a, pltpu.HBM)

    spec = keep(spectra.reshape(CH, 2, BINS))
    source_index = keep(source_index)
    half_table = (CHUNKS // 2, 2 * CB, LAGS)
    raw = pltpu.VMEM((CH, 2, HALF), BF)
    other, x, factors = call(
        other_kernel,
        [shaped(piece, BF), shaped((2 * CH, HALF), BF), shaped((192, LAGS), F32)],
        [hbm] * 3,
        "other",
        [raw, pltpu.SMEM((NSRC,), jnp.int32), pltpu.SemaphoreType.DMA((4,))],
    )(spec, source_index, keep(jnp.asarray(factors)))
    got = lax.ppermute(other, "core", PAIR)
    mine, table, planes, window, member = call(
        mine_kernel,
        [
            shaped(piece, BF),
            shaped(half_table, BF),
            shaped((32, BINS), F32),
            shaped((32, LAGS), F32),
            shaped((2, 32, LANE), F32),
        ],
        [hbm] * 4 + [VMEM] * 2,
        "mine",
        [
            raw,
            pltpu.SMEM((NSRC,), jnp.int32),
            pltpu.SMEM((CH,), jnp.int32),
            pltpu.SMEM((2, NSRC), jnp.int32),
            pltpu.SemaphoreType.DMA((4,)),
        ],
    )(spec, source_index, keep(interrogator), keep(lag_bounds.T), x, factors)
    parts = lax.all_to_all(mine + got, ("xlo", "z"), 0, 0)
    parts = call(spread_kernel, shaped(piece, BF), [VMEM], "spread")(parts)
    mine_half = lax.all_to_all(parts, ("xlo", "z"), 0, 0)
    other_half = lax.ppermute(mine_half, "core", PAIR)
    crosses = [pltpu.VMEM((NSRC * CH, 2 * CB), BF), pltpu.VMEM(piece, F32)]
    first = call(
        first_half_kernel, shaped((NSRC * CH, LAGS), F32), [VMEM] * 3, "first_half", crosses
    )(planes, mine_half, table)
    other_table = call(
        other_table_kernel,
        shaped(half_table, BF),
        [VMEM, pl.BlockSpec(memory_space=pl.ANY)],
        "other_table",
    )(table, first)
    other_half, other_table = lax.optimization_barrier((other_half, other_table))
    corr = call(
        second_half_kernel, shaped((8, 32, LAGS), F32), [VMEM] * 4, "second_half", crosses
    )(planes, other_half, other_table, first)
    days = lax.all_to_all(corr, ("xhi", "y"), 0, 0)
    ref, fits = call(
        drift_kernel,
        [shaped((32, LAGS), BF), shaped((2, 4, 4, 1, LANE), F32)],
        [VMEM] * 3,
        "drift",
    )(window, member, days)
    fits = lax.all_to_all(fits.reshape(32, 1, LANE), ("xhi", "xlo", "core", "y"), 0, 0)
    fits = call(repeat_sum_kernel, shaped((8, 1, LANE), F32), [VMEM], "near_fits")(fits)
    fits = lax.all_to_all(fits, "z", 0, 0)
    ref, drift = call(
        finish_kernel,
        [shaped((32, LAGS), BF), shaped((1, NINT), F32)],
        [VMEM] * 2,
        "finish",
    )(fits, ref)
    return ref.reshape(2, CH, LAGS), drift


def solution(mesh):
    fine = Mesh(mesh.devices.reshape(8, 2, 2, 2, 4), ("z", "xlo", "core", "xhi", "y"))
    chan = ("z", "xlo", "core")
    day = ("xhi", "y")
    return jax.shard_map(
        per_device,
        mesh=fine,
        in_specs=(P(day, chan, None, None), P(), P(chan), P()),
        out_specs=(P(day, chan, None), P(day, None)),
        check_vma=False,
    )
```
